32 devices in a mesh: groups: 2 (over y), img: 8 (over z, x), sub: 2 (over core).
Axes of the slice: x: 2, y: 2, z: 4, core: 2. Of those that a mesh axis runs over, the one named last changes fastest.
Arguments:
- feats: bfloat16 [16, 128, 256], P(('groups', 'img')), parts along dimension 0
- grad_msg: bfloat16 [16, 128, 256], P(('groups', 'img'), None, 'sub'), parts along dimension 0, may hold values from -6 to 6
- w_qk: bfloat16 [256, 256], P(None, 'sub'), may hold values from -0.375 to 0.375
- w_v: bfloat16 [256, 256], P(None, 'sub'), may hold values from -0.375 to 0.375
- pair_slots: int32 [16, 4, 2], P(('groups', 'img')), parts along dimension 0, may hold values from -1 to 7, as said below
- counts: int32 [16], P(('groups', 'img')), parts along dimension 0, may hold values from 32 to 128, as said below
Outputs:
- grad_feats: bfloat16 [16, 128, 256], P(('groups', 'img'), None, 'sub'), parts along dimension 0
- grad_weights: float32 [4, 256, 256], P('groups', 'img', 'sub'), parts along dimension 0
The draws below stay inside these ranges and needn't reach their ends.
There are 2 independent parts, one for each index of `groups`. The reference program is written for one: setup_inputs(seed, part) draws one part's arguments, and reference() takes and returns one part's arrays. A program takes and returns all parts, laid end to end along the dimension named above; an argument that names none is the same for every part. Nothing has to cross between parts.
Inputs may be any that keep to these rules, and one draw needn't show every extreme that they name: `pair_slots`: row o lists the pairs owned by index o of img: (i, j) with i != j first, its remaining slots -1; 9 pairs in all; some owner lists exactly 4 pairs. `counts`: some image has all 128 keypoints.
All inputs are finite; a program needn't handle non-finite values.
Results may differ from the reference program's by a relative error of at most 0.012.
Values may be sent and summed in bfloat16 or wider, within the bound.
A program may use at most 64 MiB of HBM per device.

```python
import jax
import jax.numpy as jnp
from jax import lax

D = 256
HEAD_DIM = 64
KP = 128
PMAX = 4
IMAGES = 8
PAIRS = 9


def draw_feats(key, part):
    base_key = jax.random.fold_in(jax.random.fold_in(key, 3), 0)
    values = jax.random.normal(base_key, (IMAGES, KP, D), jnp.float32)
    return values.astype(jnp.bfloat16)


def draw_counts(key, part):
    size_key, full_key = jax.random.split(jax.random.fold_in(key, 5))
    sizes = jax.random.randint(size_key, (IMAGES,), KP // 4, KP + 1)
    fullest = jax.random.randint(full_key, (), 0, IMAGES)
    return sizes.at[fullest].set(KP).astype(jnp.int32)


def draw_pair_slots(key, part):
    keys = jax.random.split(jax.random.fold_in(key, 7), 5)
    left = jax.random.randint(keys[0], (PAIRS,), 0, IMAGES)
    right = (left + jax.random.randint(keys[1], (PAIRS,), 1, IMAGES)) % IMAGES
    busy = jax.random.randint(keys[2], (), 0, IMAGES)
    others = (jnp.arange((IMAGES - 1) * PMAX, dtype=jnp.int32) // PMAX + busy + 1) % IMAGES
    others = jax.random.permutation(keys[3], others)[:PAIRS - PMAX]
    owner = jnp.concatenate([jnp.full((PMAX,), busy, jnp.int32), others.astype(jnp.int32)])
    owner = jax.random.permutation(keys[4], owner)
    same = owner[:, None] == owner[None, :]
    earlier = jnp.arange(PAIRS)[None, :] < jnp.arange(PAIRS)[:, None]
    slot = jnp.sum((same & earlier).astype(jnp.int32), axis=1)
    table = jnp.full((IMAGES * PMAX, 2), -1, jnp.int32)
    table = table.at[owner * PMAX + slot].set(jnp.stack([left, right], axis=1).astype(jnp.int32))
    return table.reshape(IMAGES, PMAX, 2)


def block_scale(rng, shape, cuts, least, high):
    loudness = 1.0
    for position, shards_of in cuts:
        draws = jax.random.uniform(jax.random.fold_in(jax.random.fold_in(rng, 6), position), (shards_of,), jnp.float32, least / len(cuts), high / len(cuts))
        loudness = loudness * jnp.repeat(jnp.exp(draws), shape[position] // shards_of).reshape((-1,) + (1,) * (len(shape) - 1 - position))
    return loudness


def gaussian(stream_key, shape, scale, bound, cuts=(), kind=jnp.bfloat16):
    result = scale * jax.random.normal(stream_key, shape, jnp.float32)
    if cuts:
        result = result * block_scale(stream_key, shape, cuts, -0.22, 0.18)
    return jnp.clip(result, -bound, bound).astype(kind)


def setup_inputs(seed: int = 0, part: int = 0) -> dict:
    streams_of = jax.random.split(jax.random.key(seed), 7)
    part_keys = jax.random.split(jax.random.fold_in(streams_of[6], part), 7)
    feats = draw_feats(jax.random.fold_in(jax.random.fold_in(streams_of[6], part), 71), part)
    grad_msg = gaussian(part_keys[1], (IMAGES, KP, D), 1.0, 6.0, ((0, 8), (2, 2)))
    w_qk = gaussian(streams_of[2], (D, D), D ** -0.5, 0.375, ((1, 2),))
    w_v = gaussian(streams_of[3], (D, D), D ** -0.5, 0.375, ((1, 2),))
    pair_slots = draw_pair_slots(jax.random.fold_in(jax.random.fold_in(streams_of[6], part), 71), part)
    counts = draw_counts(jax.random.fold_in(jax.random.fold_in(streams_of[6], part), 71), part)
    return dict(feats=feats, grad_msg=grad_msg, w_qk=w_qk, w_v=w_v, pair_slots=pair_slots, counts=counts)


NEG_FILL = -1.0e30


def contract(left, right, left_dim, right_dim):
    return lax.dot_general(left, right, (((left_dim,), (right_dim,)), ((), ())), preferred_element_type=jnp.float32)


def normalize(scores, axis):
    top = jnp.max(scores, axis=axis, keepdims=True)
    weights = jnp.exp(scores - top)
    return weights / jnp.sum(weights, axis=axis, keepdims=True)


def head_backward(parts, scale):
    q_left, v_left, g_left, q_right, v_right, g_right, m_left, m_right = parts
    scores = contract(q_left, q_right, 1, 1) * scale
    row_probs = normalize(jnp.where(m_right[None, :] > 0, scores, NEG_FILL), 1)
    col_probs = normalize(jnp.where(m_left[:, None] > 0, scores, NEG_FILL), 0)
    gm_left = g_left * m_left[:, None]
    gm_right = g_right * m_right[:, None]
    row_low = row_probs.astype(jnp.bfloat16)
    col_low = col_probs.astype(jnp.bfloat16)
    dv_right = contract(row_low, gm_left, 0, 0)
    dv_left = contract(col_low, gm_right, 1, 0)
    drow = contract(gm_left, v_right, 1, 1)
    dcol = contract(v_left, gm_right, 1, 1)
    dscore = row_probs * (drow - jnp.sum(drow * row_probs, axis=1, keepdims=True))
    dscore = dscore + col_probs * (dcol - jnp.sum(dcol * col_probs, axis=0, keepdims=True))
    dscore_low = (dscore * scale).astype(jnp.bfloat16)
    dq_left = contract(dscore_low, q_right, 1, 0)
    dq_right = contract(dscore_low, q_left, 0, 0)
    return dq_left, dv_left, dq_right, dv_right


def slot_backward(block, mask):
    width = block.shape[-1] // 3
    local_heads = width // HEAD_DIM
    rows = block.shape[1]

    def heads_first(part):
        return part.reshape(rows, local_heads, HEAD_DIM).transpose(1, 0, 2)

    pieces = tuple(heads_first(block[side, :, kind * width:(kind + 1) * width]) for side in range(2) for kind in range(3))

    def one_head(item):
        return head_backward(item + (mask[0], mask[1]), HEAD_DIM ** -0.5)

    dq_left, dv_left, dq_right, dv_right = lax.map(one_head, pieces)

    def heads_last(part):
        return part.transpose(1, 0, 2).reshape(rows, width)

    left = jnp.concatenate([heads_last(dq_left), heads_last(dv_left)], axis=1)
    right = jnp.concatenate([heads_last(dq_right), heads_last(dv_right)], axis=1)
    return jnp.stack([left, right]).astype(jnp.bfloat16)


def reference(feats, grad_msg, w_qk, w_v, pair_slots, counts):
    images, rows, width = feats.shape
    flat_feats = feats.reshape(images * rows, width)
    query_keys = jnp.dot(flat_feats, w_qk, preferred_element_type=jnp.float32).astype(jnp.bfloat16).reshape(images, rows, width)
    values = jnp.dot(flat_feats, w_v, preferred_element_type=jnp.float32).astype(jnp.bfloat16).reshape(images, rows, width)
    packed = jnp.concatenate([query_keys, values, grad_msg], axis=2)
    flat = pair_slots.reshape(-1, 2)
    live = flat[:, 0] >= 0
    order = jnp.cumsum(live.astype(jnp.int32)) - 1
    target = jnp.where(live, order, PAIRS).astype(jnp.int32)
    chosen = jnp.zeros((PAIRS + 1, 2), jnp.int32).at[target].set(flat)[:PAIRS]
    positions = jnp.arange(rows, dtype=jnp.int32)

    def step(totals, pair):
        left = pair[0]
        right = pair[1]
        block = jnp.stack([packed[left], packed[right]])
        mask = jnp.stack([positions < counts[left], positions < counts[right]]).astype(jnp.bfloat16)
        grads = slot_backward(block, mask).astype(jnp.float32)
        totals = totals.at[left].add(grads[0])
        totals = totals.at[right].add(grads[1])
        return totals, None

    totals, _ = lax.scan(step, jnp.zeros((images, rows, 2 * width), jnp.float32), chosen)
    grad_qk = totals[:, :, :width].astype(jnp.bfloat16).reshape(-1, width)
    grad_v = totals[:, :, width:].astype(jnp.bfloat16).reshape(-1, width)
    grad_feats = jnp.dot(grad_qk, w_qk.T, preferred_element_type=jnp.float32) + jnp.dot(grad_v, w_v.T, preferred_element_type=jnp.float32)
    grad_feats = grad_feats.astype(jnp.bfloat16).reshape(images, rows, width)
    grad_weights = jnp.stack([contract(flat_feats, grad_qk, 0, 0), contract(flat_feats, grad_v, 0, 0)])
    return grad_feats, grad_weights
```

```python
import functools

import jax
import jax.numpy as jnp
from jax import lax
from jax.experimental import pallas as pl
from jax.experimental.pallas import tpu as pltpu
from jax.sharding import PartitionSpec as P

HEAD_DIM = 64
NEG_FILL = -1e30
LANES = 128
MESH = pl.DeviceIdType.MESH
HBM = pl.BlockSpec(memory_space=pltpu.HBM)
VMEM = pl.BlockSpec(memory_space=pltpu.VMEM)


def contract(left, right, left_dim, right_dim):
    return lax.dot_general(
        left, right, (((left_dim,), (right_dim,)), ((), ())), preferred_element_type=jnp.float32
    )


def loop(low, high, body):
    def step(d, carry):
        body(d)
        return carry

    lax.fori_loop(low, high, step, 0)


def static_loop(low, high, body):
    if high - low <= 8:
        for d in range(low, high):
            body(d)
    else:
        loop(low, high, body)


def kernel(
    n, feats, grad, w_qk_in, w_v_in, pairs, counts, grad_feats, grad_weights,
    feats_own, grad_own, feats_in, grad_in, pair_own, count_own, table, weights,
    turn, q_rows, v_rows, q_heads, g_heads, q_turned, g_turned, feats_turned, total_turned, product,
    terms, outgoing, arrived, term_own, term_out, term_in, swap_out, swap_in,
    local_sem, ready, f_send, g_send, c_send, f_recv, g_recv, c_recv, t_send, t_recv,
    w_send, w_recv, d_send, d_recv, s_sem,
):
    me = lax.axis_index("img")
    sub = lax.axis_index("sub")
    columns = n // 2
    z, x = me // 2, lax.rem(me, 2)
    rows = feats.shape[1]
    half = rows // 2
    width = w_qk_in.shape[1]
    heads = width // HEAD_DIM
    scale = HEAD_DIM ** (-0.5)
    share = terms.shape[1]
    depth = feats.shape[2]
    low = jnp.bfloat16
    mine = pl.ds(pl.multiple_of(sub * half, half), half)
    other = pl.ds(pl.multiple_of((1 - sub) * half, half), half)
    beside = me + 1 - 2 * x
    across = {"img": beside}
    partner = {"sub": 1 - sub}
    last = n - 1
    first_k, end_k = x, columns - z

    barrier = pltpu.get_barrier_semaphore()
    pl.semaphore_signal(barrier, inc=1, device_id=partner, device_id_type=MESH)
    loop(me + 1, n, lambda j: pl.semaphore_signal(
        barrier, inc=1, device_id={"img": j}, device_id_type=MESH
    ))
    own = [
        pltpu.make_async_copy(pairs.at[0], pair_own, local_sem.at[0]),
        pltpu.make_async_copy(counts, count_own, local_sem.at[1]),
        pltpu.make_async_copy(feats.at[0], feats_own, local_sem.at[2]),
        pltpu.make_async_copy(w_qk_in, weights.at[:, pl.ds(0, width)], local_sem.at[3]),
        pltpu.make_async_copy(w_v_in, weights.at[:, pl.ds(width, width)], local_sem.at[4]),
        pltpu.make_async_copy(grad.at[0], grad_own, local_sem.at[5]),
    ]
    for copy in own:
        copy.start()
    pl.semaphore_wait(barrier, me + 1)

    def push(src, dst, send, recv, device):
        return pltpu.make_async_remote_copy(
            src_ref=src, dst_ref=dst, send_sem=send, recv_sem=recv,
            device_id=device, device_id_type=MESH,
        )

    def ship_feats(d, device):
        return push(feats.at[0, mine], feats_in.at[d, mine], f_send.at[d], f_recv.at[d], device)

    def ship_grad(d, device):
        return push(grad.at[0], grad_in.at[d], g_send.at[d], g_recv.at[d], device)

    def ship(d, device):
        ship_feats(d, device).start()
        ship_grad(d, device).start()

    def sent(d, device):
        ship_feats(d, device).wait_send()
        ship_grad(d, device).wait_send()

    def below(d):
        return {"img": me - 2 * d}

    def core(d, half_rows):
        return push(
            feats_in.at[d, half_rows], feats_in.at[d, half_rows], c_send.at[d], c_recv.at[d], partner
        )

    def table_copy(j):
        return push(table.at[me], table.at[me], t_send.at[j], t_recv.at[me], {"img": j})

    def table_wait(j):
        push(table.at[j], table.at[j], t_send.at[j], t_recv.at[j], {"img": j}).wait_recv()

    @pl.when(me < last)
    def _():
        loop(0, me, lambda j: pl.semaphore_signal(
            ready.at[me], inc=1, device_id={"img": j}, device_id_type=MESH
        ))

    own[0].wait()
    own[1].wait()
    left, right = pair_own[0:1, :], pair_own[1:2, :]
    count_a = jnp.full((1, LANES), count_own[0], jnp.int32)
    table[me] = jnp.concatenate([jnp.full((1, LANES), -1, jnp.int32), count_a], axis=0)
    table[me, 0:1, 0 : pairs.shape[2]] = jnp.where(left >= 0, left * n + right, -1)
    loop(0, me, lambda j: table_copy(j).start())
    @pl.when(x == 1)
    def _():
        ship(0, across)

    @pl.when(z > 0)
    def _():
        ship(z, below(z))


    row_ids = lax.broadcasted_iota(jnp.int32, (rows, width), 0)
    sublane_ids = lax.broadcasted_iota(jnp.int32, (rows, rows), 0)
    unit = lax.broadcasted_iota(jnp.int32, (depth, depth), 0) == lax.broadcasted_iota(jnp.int32, (depth, depth), 1)
    unit = jnp.where(unit, 1.0, 0.0).astype(low)

    def stack(part):
        head = lax.broadcasted_iota(jnp.int32, part.shape, 1) // HEAD_DIM
        zero = jnp.zeros((), part.dtype)
        return [jnp.where(head == h, part, zero) for h in range(heads)]

    def project(block, cotangent, count):
        projected = contract(block, weights[...], 1, 0)
        q = projected[:, :width].astype(low)
        g = jnp.where(row_ids < count, cotangent, jnp.zeros((), low))
        turned = contract(turn[...], block, 1, 1).astype(low)
        g_t = contract(unit[:width, :width], g, 1, 1).astype(low)
        return q, projected[:, width:].astype(low), g, turned[:width], g_t, turned[width:]

    def keep(a, block, cotangent, count):
        q, v, g, q_t, g_t, f_t = project(block, cotangent, count)
        part = slice(a * rows, (a + 1) * rows)
        q = (q.astype(jnp.float32) * scale).astype(low)
        q_rows[part], v_rows[part] = q, v
        for h, (q_part, g_part) in enumerate(zip(stack(q), stack(g))):
            spot = slice((2 * h + a) * rows, (2 * h + a + 1) * rows)
            q_heads[spot], g_heads[spot] = q_part, g_part
        q_turned[:, part], g_turned[:, part], feats_turned[:, part] = q_t, g_t, f_t

    for copy in own[2:]:
        copy.wait()

    @pl.when(me < last)
    def _():
        turn[0:width] = contract(unit, weights[:, 0:width], 1, 0).astype(low).T
        turn[width:] = unit
        keep(0, feats_own[...], grad_own[...], count_a)
        total_turned[...] = jnp.zeros_like(total_turned)
        product[...] = jnp.zeros_like(product)

    arrived[last] = jnp.zeros(arrived.shape[1:], low)

    @pl.when((x == 0) & (me < last - 1))
    def _():
        pl.semaphore_wait(ready.at[me + 1], 1)
        table_copy(me + 1).start()
        ship(0, across)

    @pl.when(z > 1)
    def _():
        sent(z, below(z))
        loop(1, z, lambda d: ship(d, below(d)))

    def answer(j):
        @pl.when(j < last)
        def _():
            pl.semaphore_wait(ready.at[j], 1)
            table_copy(j).start()

    def times(a, k):
        image = me if a == 0 else beside
        peer = jnp.where(k == 0, beside, me + 2 * k)
        listed = table[:, 0, :]
        hits = (listed == image * n + peer) | (listed == peer * n + image)
        return jnp.sum(hits.astype(jnp.float32), keepdims=True)

    def side(scores, slope, live, factor):
        masked = jnp.where(live, scores, NEG_FILL)
        e = jnp.exp(masked - jnp.max(masked, axis=0, keepdims=True))
        inverse = 1.0 / jnp.sum(e, axis=0, keepdims=True)
        weighted = slope * e
        mean = jnp.sum(weighted, axis=0, keepdims=True) * inverse
        inverse = inverse * factor
        d = (weighted - e * mean) * (inverse * scale)
        return (e * inverse).astype(low), d.astype(low)

    def weight_copy(j):
        return push(outgoing.at[j], arrived.at[me], w_send.at[j], w_recv.at[me], {"img": j})

    def term_copy(k, s):
        device = {"img": jnp.where(k == 0, beside, me + 2 * k), "sub": s}
        return push(term_out.at[k, s], term_in.at[k, sub], d_send.at[k, s], d_recv.at[k, sub], device)

    swap = push(swap_out.at[1 - sub], swap_in, s_sem.at[0], s_sem.at[1], partner)

    def each_other(body):
        loop(1, n, lambda d: body(lax.rem(me + d, n)))

    def term_of(total):
        return contract(weights[...], total, 1, 0)

    def send_term(k, total):
        term = term_of(total)
        for s in range(2):
            term_out[k, s] = term[s * width : (s + 1) * width].astype(low)
            term_copy(k, s).start()

    def work(k):
        peer = jnp.where(k == 0, beside, me + 2 * k)

        @pl.when(k > 0)
        def _():
            ship_feats(k, across).wait_recv()
            core(k, mine).start()
            ship_grad(k, across).wait_recv()
            core(k, other).wait_recv()

        count_c = table[peer, 1:2, :]
        count_b = table[beside, 1:2, :]
        block = feats_in[k]
        q, v, g, q_t, g_t, f_t = project(block, grad_in[k], count_c)
        scores = contract(q_rows[...], jnp.concatenate(stack(q), axis=0), 1, 1)
        slopes = contract(v_rows[...], jnp.concatenate(stack(g), axis=0), 1, 1)
        scores_t = contract(q, q_heads[...], 1, 1)
        slopes_t = contract(v, g_heads[...], 1, 1)
        factors = [times(a, k) for a in range(2)]
        col_live = sublane_ids < count_c
        row_live = [sublane_ids < count_a, sublane_ids < count_b]
        x_q, x_v, y_q, y_v = [], [], [], []
        for h in range(heads):
            cols = [side(
                scores[a * rows : (a + 1) * rows, h * rows : (h + 1) * rows],
                slopes[a * rows : (a + 1) * rows, h * rows : (h + 1) * rows],
                row_live[a], factors[a],
            ) for a in range(2)]
            spots = [slice((2 * h + a) * rows, (2 * h + a + 1) * rows) for a in range(2)]
            tops = [side(scores_t[:, spots[a]], slopes_t[:, spots[a]], col_live, factors[a]) for a in range(2)]
            col, dcol = [jnp.concatenate(parts, axis=0) for parts in zip(*cols)]
            row_t, drow_t = [jnp.concatenate(parts, axis=1) for parts in zip(*tops)]
            mine_h = slice(h * HEAD_DIM, (h + 1) * HEAD_DIM)
            q_a, g_a = q_turned[mine_h], g_turned[mine_h]
            q_c, g_c = q_t[mine_h], g_t[mine_h]
            x_q.append(contract(q_c, dcol, 1, 1) + contract(q_c, drow_t, 1, 0))
            x_v.append(contract(g_c, col, 1, 1))
            y_q.append(contract(q_a, dcol, 1, 0) + contract(q_a, drow_t, 1, 1))
            y_v.append(contract(g_a, row_t, 1, 1))
        x_t = jnp.concatenate(x_q + x_v, axis=0)
        y_t = jnp.concatenate(y_q + y_v, axis=0)
        y_low = y_t.astype(low)
        product[...] += contract(feats_turned[...], x_t.astype(low), 1, 1) + contract(f_t, y_low, 1, 1)

        @pl.when(k == end_k - 1)
        def _():
            for c in range(n):
                piece = product[c * share : (c + 1) * share]
                terms[c] = piece
                outgoing[c] = piece.astype(low)
            each_other(lambda j: weight_copy(j).start())

        total_turned[...] += x_t

        @pl.when(k == 0)
        def _():
            total_turned[:, rows:] += y_t

        @pl.when(k > 0)
        def _():
            send_term(k, y_low)

    @pl.when(me < last)
    def _():
        ship_feats(0, across).wait_recv()
        core(0, mine).start()
        loop((z + 1) * 2, n, answer)
        table_wait(beside)
        ship_grad(0, across).wait_recv()
        core(0, other).wait_recv()
        keep(1, feats_in[0], grad_in[0], table[beside, 1:2, :])
        loop((z + 1) * 2, n, table_wait)
        loop(0, z * 2, table_wait)
        loop(first_k, end_k, work)
        send_term(0, total_turned[:, rows:].astype(low))
        term = term_of(total_turned[:, :rows].astype(low))
        for s in range(2):
            term_own[s] = term[s * width : (s + 1) * width]
            swap_out[s] = term_own[s].astype(low)
        swap.start()

    @pl.when(me == last)
    def _():
        terms[last] = jnp.zeros(terms.shape[1:], jnp.float32)
        term_own[...] = jnp.zeros_like(term_own)
        swap_in[...] = jnp.zeros_like(swap_in)

    @pl.when(me < last)
    def _():
        swap.wait_recv()

    def came(k):
        return [
            push(term_out.at[k, s], term_in.at[k, s], d_send.at[k, s], d_recv.at[k, s], across)
            for s in range(2)
        ]

    def take(k):
        for copy in came(k):
            copy.wait_recv()
        term_own[sub] += term_in[k, 0].astype(jnp.float32) + term_in[k, 1].astype(jnp.float32)

    @pl.when(beside < last)
    def _():
        take(0)

    loop(1, z + 1, take)
    grad_feats[0] = (term_own[sub] + swap_in[...].astype(jnp.float32)).T.astype(grad_feats.dtype)

    def weight_wait(j):
        @pl.when(j < last)
        def _():
            push(outgoing.at[j], arrived.at[j], w_send.at[j], w_recv.at[j], across).wait_recv()

    each_other(weight_wait)
    total = terms[me]
    for d in range(1, n):
        total = total + arrived[lax.rem(me + d, n)].astype(jnp.float32)
    grad_weights[0] = total[:, :width]
    grad_weights[1] = total[:, width:]

    @pl.when(z > 0)
    def _():
        loop(1, jnp.maximum(z, 2), lambda d: sent(d, below(d)))

    loop(0, me, lambda j: table_copy(j).wait_send())

    @pl.when((x == 1) | (me < last - 1))
    def _():
        sent(0, across)

    @pl.when((x == 0) & (me < last - 1))
    def _():
        table_copy(me + 1).wait_send()

    @pl.when(me < last)
    def _():
        core(0, mine).wait_send()
        loop(1, end_k, lambda k: core(k, mine).wait_send())
        loop((z + 1) * 2, last, lambda j: table_copy(j).wait_send())
        each_other(lambda j: weight_copy(j).wait_send())
        swap.wait_send()

        def terms_sent(k):
            for s in range(2):
                term_copy(k, s).wait_send()

        loop(0, end_k, terms_sent)


def local(feats, grad_msg, w_qk, w_v, pair_slots, counts):
    n = lax.axis_size("img")
    columns = n // 2
    rows, depth = feats.shape[1:]
    width = w_qk.shape[1]
    heads = width // HEAD_DIM
    share = depth // n
    slots = pair_slots.shape[1]
    low, full = jnp.bfloat16, jnp.float32
    vmem = pltpu.VMEM
    dma = pltpu.SemaphoreType.DMA
    return pl.pallas_call(
        functools.partial(kernel, n),
        out_shape=(
            vmem((1, rows, width), low),
            vmem((2, share, width), full),
        ),
        in_specs=[HBM] * 6,
        out_specs=(VMEM,) * 2,
        scratch_shapes=[
            vmem((rows, depth), low),
            vmem((rows, width), low),
            vmem((columns, rows, depth), low),
            vmem((columns, rows, width), low),
            vmem((2, slots), jnp.int32),
            pltpu.SMEM((1,), jnp.int32),
            vmem((n, 2, LANES), jnp.int32),
            vmem((depth, 2 * width), low),
            vmem((width + depth, depth), low),
            vmem((2 * rows, width), low),
            vmem((2 * rows, width), low),
            vmem((2 * heads * rows, width), low),
            vmem((2 * heads * rows, width), low),
            vmem((width, 2 * rows), low),
            vmem((width, 2 * rows), low),
            vmem((depth, 2 * rows), low),
            vmem((2 * width, 2 * rows), full),
            vmem((depth, 2 * width), full),
            vmem((n, share, 2 * width), full),
            vmem((n, share, 2 * width), low),
            vmem((n, share, 2 * width), low),
            vmem((2, width, rows), full),
            vmem((columns, 2, width, rows), low),
            vmem((columns, 2, width, rows), low),
            vmem((2, width, rows), low),
            vmem((width, rows), low),
            dma((6,)), pltpu.SemaphoreType.REGULAR((n,)),
            dma((columns,)), dma((columns,)), dma((columns,)),
            dma((columns,)), dma((columns,)), dma((columns,)),
            dma((n,)), dma((n,)), dma((n,)), dma((n,)),
            dma((columns, 2)), dma((columns, 2)), dma((2,)),
        ],
        compiler_params=pltpu.CompilerParams(
            collective_id=0, has_side_effects=True, vmem_limit_bytes=60 * 1024 * 1024
        ),
        name="backward",
    )(feats, grad_msg, w_qk, w_v, jnp.transpose(pair_slots, (0, 2, 1)), counts)


def solution(mesh):
    in_specs = (
        P(("groups", "img"), None, None),
        P(("groups", "img"), None, "sub"),
        P(None, "sub"),
        P(None, "sub"),
        P(("groups", "img"), None, None),
        P(("groups", "img")),
    )
    out_specs = (P(("groups", "img"), None, "sub"), P("groups", "img", "sub"))
    return jax.shard_map(local, mesh=mesh, in_specs=in_specs, out_specs=out_specs, check_vma=False)
```

```python
import functools

import jax
import jax.numpy as jnp
from jax import lax
from jax.experimental import pallas as pl
from jax.experimental.pallas import tpu as pltpu
from jax.sharding import PartitionSpec as P

HEAD_DIM = 64
NEG_FILL = -1e30
LANES = 128
HELD_COLUMNS = 8
MESH = pl.DeviceIdType.MESH
HBM = pl.BlockSpec(memory_space=pltpu.HBM)
VMEM = pl.BlockSpec(memory_space=pltpu.VMEM)


def contract(left, right, left_dim, right_dim):
    return lax.dot_general(
        left, right, (((left_dim,), (right_dim,)), ((), ())), preferred_element_type=jnp.float32
    )


def loop(low, high, body):
    def step(d, carry):
        body(d)
        return carry

    lax.fori_loop(low, high, step, 0)


def static_loop(low, high, body):
    if high - low <= 8:
        for d in range(low, high):
            body(d)
    else:
        loop(low, high, body)


def kernel(
    n, feats, grad, w_qk_in, w_v_in, pairs, counts, grad_feats, grad_weights,
    feats_own, grad_own, feats_in, grad_in, pair_own, count_own, table, weights,
    turn, q_rows, v_rows, q_heads, g_heads, q_turned, g_turned, feats_turned, total_turned, product,
    cols, dcols, rows_t, drows_t, peer_q, peer_g, peer_feats,
    terms, outgoing, arrived, term_own, term_half, term_out, term_in, swap_out, swap_in,
    local_sem, ready, f_send, g_send, c_send, f_recv, g_recv, c_recv, t_send, t_recv,
    w_send, w_recv, d_send, d_recv, s_send, s_recv,
):
    me = lax.axis_index("img")
    sub = lax.axis_index("sub")
    columns = n // 2
    held = columns <= HELD_COLUMNS
    z, x = me // 2, lax.rem(me, 2)
    rows = feats.shape[1]
    half = rows // 2
    width = w_qk_in.shape[1]
    heads = width // HEAD_DIM
    scale = HEAD_DIM ** (-0.5)
    share = terms.shape[1]
    depth = feats.shape[2]
    low = jnp.bfloat16
    mine = pl.ds(pl.multiple_of(sub * half, half), half)
    other = pl.ds(pl.multiple_of((1 - sub) * half, half), half)
    beside = me + 1 - 2 * x
    across = {"img": beside}
    partner = {"sub": 1 - sub}
    reach = columns // 2

    def span(column):
        return reach - 1 + jnp.where(column < reach, 1, 0)

    def peer_of(k):
        return jnp.where(k == 0, beside, lax.rem(z + k, columns) * 2 + x)

    def target_of(k):
        return lax.rem(z - k + columns, columns) * 2 + x

    def targets(low_k, high_k, body):
        def one(k):
            @pl.when(k <= span(lax.rem(z - k + columns, columns)))
            def _():
                body(k)

        loop(low_k, high_k, one)

    first_k, end_k = x, span(z) + 1

    barrier = pltpu.get_barrier_semaphore()
    pl.semaphore_signal(barrier, inc=1, device_id=partner, device_id_type=MESH)
    loop(me + 1, n, lambda j: pl.semaphore_signal(
        barrier, inc=1, device_id={"img": j}, device_id_type=MESH
    ))
    own = [
        pltpu.make_async_copy(pairs.at[0], pair_own, local_sem.at[0]),
        pltpu.make_async_copy(counts, count_own, local_sem.at[1]),
        pltpu.make_async_copy(feats.at[0], feats_own, local_sem.at[2]),
        pltpu.make_async_copy(w_qk_in, weights.at[:, pl.ds(0, width)], local_sem.at[3]),
        pltpu.make_async_copy(w_v_in, weights.at[:, pl.ds(width, width)], local_sem.at[4]),
        pltpu.make_async_copy(grad.at[0], grad_own, local_sem.at[5]),
    ]
    for copy in own:
        copy.start()
    pl.semaphore_wait(barrier, me + 1)

    def push(src, dst, send, recv, device):
        return pltpu.make_async_remote_copy(
            src_ref=src, dst_ref=dst, send_sem=send, recv_sem=recv,
            device_id=device, device_id_type=MESH,
        )

    def ship_feats(d, device):
        return push(feats.at[0, mine], feats_in.at[d, mine], f_send.at[d], f_recv.at[d], device)

    def ship_grad(d, device):
        return push(grad.at[0], grad_in.at[d], g_send.at[d], g_recv.at[d], device)

    def ship(d, device):
        ship_feats(d, device).start()
        ship_grad(d, device).start()

    def sent(d, device):
        ship_feats(d, device).wait_send()
        ship_grad(d, device).wait_send()

    def toward(k):
        return {"img": target_of(k)}

    def core(d, half_rows):
        return push(
            feats_in.at[d, half_rows], feats_in.at[d, half_rows], c_send.at[d], c_recv.at[d], partner
        )

    def table_copy(j):
        return push(table.at[me], table.at[me], t_send.at[j], t_recv.at[me], {"img": j})

    def table_wait(j):
        push(table.at[j], table.at[j], t_send.at[j], t_recv.at[j], {"img": j}).wait_recv()

    loop(0, me, lambda j: pl.semaphore_signal(
        ready.at[me], inc=1, device_id={"img": j}, device_id_type=MESH
    ))
    own[0].wait()
    own[1].wait()
    left, right = pair_own[0:1, :], pair_own[1:2, :]
    count_a = jnp.full((1, LANES), count_own[0], jnp.int32)
    table[me] = jnp.concatenate([jnp.full((1, LANES), -1, jnp.int32), count_a], axis=0)
    table[me, 0:1, 0 : pairs.shape[2]] = jnp.where(left >= 0, left * n + right, -1)
    loop(0, me, lambda j: table_copy(j).start())

    targets(1, jnp.minimum(z, reach) + 1, lambda k: ship(k, toward(k)))

    @pl.when(x == 1)
    def _():
        ship(0, across)


    row_ids = lax.broadcasted_iota(jnp.int32, (rows, width), 0)
    sublane_ids = lax.broadcasted_iota(jnp.int32, (rows, rows), 0)
    unit = lax.broadcasted_iota(jnp.int32, (depth, depth), 0) == lax.broadcasted_iota(jnp.int32, (depth, depth), 1)
    unit = jnp.where(unit, 1.0, 0.0).astype(low)

    def stack(part):
        head = lax.broadcasted_iota(jnp.int32, part.shape, 1) // HEAD_DIM
        zero = jnp.zeros((), part.dtype)
        return [jnp.where(head == h, part, zero) for h in range(heads)]

    def project(block, cotangent, count):
        projected = contract(block, weights[...], 1, 0)
        q = projected[:, :width].astype(low)
        g = jnp.where(row_ids < count, cotangent, jnp.zeros((), low))
        turned = contract(turn[...], block, 1, 1).astype(low)
        g_t = contract(unit[:width, :width], g, 1, 1).astype(low)
        return q, projected[:, width:].astype(low), g, turned[:width], g_t, turned[width:]

    def keep(a, block, cotangent, count):
        q, v, g, q_t, g_t, f_t = project(block, cotangent, count)
        part = slice(a * rows, (a + 1) * rows)
        q = (q.astype(jnp.float32) * scale).astype(low)
        q_rows[part], v_rows[part] = q, v
        for h, (q_part, g_part) in enumerate(zip(stack(q), stack(g))):
            spot = slice((2 * h + a) * rows, (2 * h + a + 1) * rows)
            q_heads[spot], g_heads[spot] = q_part, g_part
        q_turned[:, part], g_turned[:, part], feats_turned[:, part] = q_t, g_t, f_t

    for copy in own[2:]:
        copy.wait()

    if n > 1:
        turn[0:width] = contract(unit, weights[:, 0:width], 1, 0).astype(low).T
        turn[width:] = unit
        keep(0, feats_own[...], grad_own[...], count_a)
        total_turned[...] = jnp.zeros_like(total_turned)
        product[...] = jnp.zeros_like(product)

    def greet(j):
        pl.semaphore_wait(ready.at[j], 1)

        @pl.when(j == beside)
        def _():
            ship(0, across)

        k = z - j // 2 + columns

        @pl.when((lax.rem(j, 2) == x) & (k <= span(j // 2)))
        def _():
            ship(k, {"img": j})

        table_copy(j).start()

    loop(me + 1, n, greet)

    def times(a, k):
        image = me if a == 0 else beside
        peer = peer_of(k)
        listed = table[:, 0, :]
        hits = (listed == image * n + peer) | (listed == peer * n + image)
        return jnp.sum(hits.astype(jnp.float32), keepdims=True)

    def side(scores, slope, live):
        masked = jnp.where(live, scores, NEG_FILL)
        e = jnp.exp(masked - jnp.max(masked, axis=0, keepdims=True))
        inverse = 1.0 / jnp.sum(e, axis=0, keepdims=True)
        weighted = slope * e
        mean = jnp.sum(weighted, axis=0, keepdims=True) * inverse
        d = (weighted - e * mean) * (inverse * scale)
        return (e * inverse).astype(low), d.astype(low)

    def weight_copy(j):
        return push(outgoing.at[j], arrived.at[me], w_send.at[j], w_recv.at[me], {"img": j})

    def term_copy(k):
        device = {"img": peer_of(k)}
        return push(term_out.at[k], term_in.at[k], d_send.at[k], d_recv.at[k], device)

    def swap(k):
        return push(swap_out.at[k], swap_in.at[k], s_send.at[k], s_recv.at[k], partner)

    def each_other(body):
        loop(1, n, lambda d: body(lax.rem(me + d, n)))

    def term_of(total):
        return contract(weights[...], total, 1, 0)

    def halve(k, total):
        term = term_of(total)
        for s in range(2):
            term_half[k, s] = term[s * width : (s + 1) * width]
        swap_out[k] = term_half[k, 1 - sub].astype(low)
        swap(k).start()

    def hand_on(k):
        swap(k).wait_recv()
        term_out[k] = (term_half[k, sub] + swap_in[k].astype(jnp.float32)).astype(low)
        term_copy(k).start()

    def slopes_of(k):
        slot = k if held else 0
        peer = peer_of(k)

        @pl.when(k > 0)
        def _():
            ship_feats(k, across).wait_recv()
            core(k, mine).start()
            if held:
                @pl.when(k < end_k - 1)
                def _():
                    table_wait(peer)
            ship_grad(k, across).wait_recv()
            core(k, other).wait_recv()

        count_c = table[peer, 1:2, :]
        count_b = table[beside, 1:2, :]
        block = feats_in[k]
        q, v, g, q_t, g_t, f_t = project(block, grad_in[k], count_c)
        scores = contract(q_rows[...], jnp.concatenate(stack(q), axis=0), 1, 1)
        slopes = contract(v_rows[...], jnp.concatenate(stack(g), axis=0), 1, 1)
        scores_t = contract(q, q_heads[...], 1, 1)
        slopes_t = contract(v, g_heads[...], 1, 1)
        peer_q[slot], peer_g[slot], peer_feats[slot] = q_t, g_t, f_t
        col_live = sublane_ids < count_c
        row_live = [sublane_ids < count_a, sublane_ids < count_b]
        for h in range(heads):
            across_h = slice(h * rows, (h + 1) * rows)
            for a in range(2):
                down = slice(a * rows, (a + 1) * rows)
                cols[slot, down, across_h], dcols[slot, down, across_h] = side(
                    scores[down, across_h], slopes[down, across_h], row_live[a]
                )
                spot = slice((2 * h + a) * rows, (2 * h + a + 1) * rows)
                rows_t[slot, :, spot], drows_t[slot, :, spot] = side(
                    scores_t[:, spot], slopes_t[:, spot], col_live
                )

    def gather_grads(k, final):
        slot = k if held else 0
        factor = jnp.concatenate(
            [jnp.broadcast_to(times(a, k), (1, rows)) for a in range(2)], axis=1
        )
        x_q, x_v, y_q, y_v = [], [], [], []
        for h in range(heads):
            head = slice(h * HEAD_DIM, (h + 1) * HEAD_DIM)
            across_h, spot = slice(h * rows, (h + 1) * rows), slice(2 * h * rows, 2 * (h + 1) * rows)
            col, dcol = cols[slot, :, across_h], dcols[slot, :, across_h]
            row_t, drow_t = rows_t[slot, :, spot], drows_t[slot, :, spot]
            q_a = (q_turned[head].astype(jnp.float32) * factor).astype(low)
            g_a = (g_turned[head].astype(jnp.float32) * factor).astype(low)
            q_c, g_c = peer_q[slot, head], peer_g[slot, head]
            x_q.append(contract(q_c, dcol, 1, 1) + contract(q_c, drow_t, 1, 0))
            x_v.append(contract(g_c, col, 1, 1))
            y_q.append(contract(q_a, dcol, 1, 0) + contract(q_a, drow_t, 1, 1))
            y_v.append(contract(g_a, row_t, 1, 1))
        x_t = jnp.concatenate(x_q + x_v, axis=0) * factor
        y_t = jnp.concatenate(y_q + y_v, axis=0)
        y_low = y_t.astype(low)

        @pl.when(k > 0)
        def _():
            halve(k, y_low)

        weight_term = contract(feats_turned[...], x_t.astype(low), 1, 1)
        weight_term = product[...] + weight_term + contract(peer_feats[slot], y_low, 1, 1)
        if final:
            for c in range(n):
                piece = weight_term[c * share : (c + 1) * share]
                terms[c] = piece
                outgoing[c] = piece.astype(low)
            each_other(lambda j: weight_copy(j).start())
        else:
            product[...] = weight_term
        total_turned[...] += x_t

        @pl.when(k == 0)
        def _():
            total_turned[:, rows:] += y_t

    if n > 1:
        ship_feats(0, across).wait_recv()
        core(0, mine).start()
        table_wait(beside)
        ship_grad(0, across).wait_recv()
        core(0, other).wait_recv()
        keep(1, feats_in[0], grad_in[0], table[beside, 1:2, :])

        def every_table():
            def one(d):
                column = lax.rem(z + d, columns)
                table_wait(column * 2 + 1 - x)
                known = (d < end_k - 1) if held else False

                @pl.when(jnp.logical_not(known))
                def _():
                    table_wait(column * 2 + x)

            loop(1, columns, one)

        if held:
            loop(first_k, end_k - 1, slopes_of)
            every_table()
            loop(first_k, end_k - 1, lambda k: gather_grads(k, False))
            loop(1, end_k - 1, hand_on)
        else:
            every_table()

            def step(k):
                slopes_of(k)
                gather_grads(k, False)

                @pl.when(k > 0)
                def _():
                    hand_on(k)

            loop(first_k, end_k - 1, step)
        slopes_of(end_k - 1)
        gather_grads(end_k - 1, True)

        @pl.when(end_k > 1)
        def _():
            hand_on(end_k - 1)

        halve(0, total_turned[:, rows:].astype(low))
        halve(columns, total_turned[:, :rows].astype(low))
        hand_on(0)
        swap(columns).wait_recv()
        term_own[...] = term_half[columns, sub] + swap_in[columns].astype(jnp.float32)

    def take(k):
        push(term_out.at[k], term_in.at[k], d_send.at[k], d_recv.at[k], across).wait_recv()
        term_own[...] += term_in[k].astype(jnp.float32)

    take(0)
    targets(1, reach + 1, take)
    grad_feats[0] = term_own[...].T.astype(grad_feats.dtype)

    def weight_wait(j):
        push(outgoing.at[j], arrived.at[j], w_send.at[j], w_recv.at[j], across).wait_recv()

    each_other(weight_wait)
    total = terms[me]
    for d in range(1, n):
        total = total + arrived[lax.rem(me + d, n)].astype(jnp.float32)
    grad_weights[0] = total[:, :width]
    grad_weights[1] = total[:, width:]

    targets(1, reach + 1, lambda k: sent(k, toward(k)))
    sent(0, across)
    if n > 1:
        each_other(lambda j: table_copy(j).wait_send())
        loop(0, end_k, lambda k: core(k, mine).wait_send())
        each_other(lambda j: weight_copy(j).wait_send())
        loop(0, end_k, lambda k: swap(k).wait_send())
        swap(columns).wait_send()
        loop(0, end_k, lambda k: term_copy(k).wait_send())


def local(feats, grad_msg, w_qk, w_v, pair_slots, counts):
    n = lax.axis_size("img")
    columns = n // 2
    held = columns if columns <= HELD_COLUMNS else 1
    rows, depth = feats.shape[1:]
    width = w_qk.shape[1]
    heads = width // HEAD_DIM
    share = depth // n
    slots = pair_slots.shape[1]
    low, full = jnp.bfloat16, jnp.float32
    vmem = pltpu.VMEM
    dma = pltpu.SemaphoreType.DMA
    return pl.pallas_call(
        functools.partial(kernel, n),
        out_shape=(
            vmem((1, rows, width), low),
            vmem((2, share, width), full),
        ),
        in_specs=[HBM] * 6,
        out_specs=(VMEM,) * 2,
        scratch_shapes=[
            vmem((rows, depth), low),
            vmem((rows, width), low),
            vmem((columns, rows, depth), low),
            vmem((columns, rows, width), low),
            vmem((2, slots), jnp.int32),
            pltpu.SMEM((1,), jnp.int32),
            vmem((n, 2, LANES), jnp.int32),
            vmem((depth, 2 * width), low),
            vmem((width + depth, depth), low),
            vmem((2 * rows, width), low),
            vmem((2 * rows, width), low),
            vmem((2 * heads * rows, width), low),
            vmem((2 * heads * rows, width), low),
            vmem((width, 2 * rows), low),
            vmem((width, 2 * rows), low),
            vmem((depth, 2 * rows), low),
            vmem((2 * width, 2 * rows), full),
            vmem((depth, 2 * width), full),
            vmem((held, 2 * rows, heads * rows), low),
            vmem((held, 2 * rows, heads * rows), low),
            vmem((held, rows, 2 * heads * rows), low),
            vmem((held, rows, 2 * heads * rows), low),
            vmem((held, width, rows), low),
            vmem((held, width, rows), low),
            vmem((held, depth, rows), low),
            vmem((n, share, 2 * width), full),
            vmem((n, share, 2 * width), low),
            vmem((n, share, 2 * width), low),
            vmem((width, rows), full),
            vmem((columns + 1, 2, width, rows), full),
            vmem((columns, width, rows), low),
            vmem((columns, width, rows), low),
            vmem((columns + 1, width, rows), low),
            vmem((columns + 1, width, rows), low),
            dma((6,)), pltpu.SemaphoreType.REGULAR((n,)),
            dma((columns,)), dma((columns,)), dma((columns,)),
            dma((columns,)), dma((columns,)), dma((columns,)),
            dma((n,)), dma((n,)), dma((n,)), dma((n,)),
            dma((columns,)), dma((columns,)), dma((columns + 1,)), dma((columns + 1,)),
        ],
        compiler_params=pltpu.CompilerParams(
            collective_id=0, has_side_effects=True, vmem_limit_bytes=60 * 1024 * 1024
        ),
        name="backward",
    )(feats, grad_msg, w_qk, w_v, jnp.transpose(pair_slots, (0, 2, 1)), counts)


def solution(mesh):
    in_specs = (
        P(("groups", "img"), None, None),
        P(("groups", "img"), None, "sub"),
        P(None, "sub"),
        P(None, "sub"),
        P(("groups", "img"), None, None),
        P(("groups", "img")),
    )
    out_specs = (P(("groups", "img"), None, "sub"), P("groups", "img", "sub"))
    return jax.shard_map(local, mesh=mesh, in_specs=in_specs, out_specs=out_specs, check_vma=False)
```

```python
import functools

import jax
import jax.numpy as jnp
from jax import lax
from jax.experimental import pallas as pl
from jax.experimental.pallas import tpu as pltpu
from jax.sharding import PartitionSpec as P

HEAD_DIM = 64
NEG_FILL = -1e30
LANES = 128
HELD_COLUMNS = 8
MESH = pl.DeviceIdType.MESH
HBM = pl.BlockSpec(memory_space=pltpu.HBM)
VMEM = pl.BlockSpec(memory_space=pltpu.VMEM)


def contract(left, right, left_dim, right_dim):
    return lax.dot_general(
        left, right, (((left_dim,), (right_dim,)), ((), ())), preferred_element_type=jnp.float32
    )


def loop(low, high, body):
    def step(d, carry):
        body(d)
        return carry

    lax.fori_loop(low, high, step, 0)


def static_loop(low, high, body):
    if high - low <= 8:
        for d in range(low, high):
            body(d)
    else:
        loop(low, high, body)


def kernel(
    n, feats, grad, w_qk_in, w_v_in, pairs, counts, grad_feats, grad_weights,
    feats_own, grad_own, feats_in, grad_in, pair_own, count_own, table, weights,
    turn, q_rows, v_rows, q_heads, g_heads, q_turned, g_turned, feats_turned, total_turned, product,
    cols, dcols, rows_t, drows_t, peer_q, peer_g, peer_feats,
    terms, outgoing, arrived, term_own, term_half, term_out, term_in, swap_out, swap_in,
    local_sem, ready, f_send, g_send, c_send, f_recv, g_recv, c_recv, t_send, t_recv,
    w_send, w_recv, d_send, d_recv, s_send, s_recv,
):
    me = lax.axis_index("img")
    sub = lax.axis_index("sub")
    columns = n // 2
    held = columns <= HELD_COLUMNS
    z, x = me // 2, lax.rem(me, 2)
    rows = feats.shape[1]
    half = rows // 2
    width = w_qk_in.shape[1]
    heads = width // HEAD_DIM
    scale = HEAD_DIM ** (-0.5)
    share = terms.shape[1]
    depth = feats.shape[2]
    low = jnp.bfloat16
    mine = pl.ds(pl.multiple_of(sub * half, half), half)
    other = pl.ds(pl.multiple_of((1 - sub) * half, half), half)
    beside = me + 1 - 2 * x
    across = {"img": beside}
    partner = {"sub": 1 - sub}
    reach = columns // 2

    def span(column):
        return reach - 1 + jnp.where(column < reach, 1, 0)

    def peer_of(k):
        return jnp.where(k == 0, beside, lax.rem(z + k, columns) * 2 + x)

    def target_of(k):
        return lax.rem(z - k + columns, columns) * 2 + x

    def targets(low_k, high_k, body):
        def one(k):
            @pl.when(k <= span(lax.rem(z - k + columns, columns)))
            def _():
                body(k)

        loop(low_k, high_k, one)

    first_k, end_k = x, span(z) + 1

    barrier = pltpu.get_barrier_semaphore()
    pl.semaphore_signal(barrier, inc=1, device_id=partner, device_id_type=MESH)
    loop(me + 1, n, lambda j: pl.semaphore_signal(
        barrier, inc=1, device_id={"img": j}, device_id_type=MESH
    ))
    own = [
        pltpu.make_async_copy(pairs.at[0], pair_own, local_sem.at[0]),
        pltpu.make_async_copy(counts, count_own, local_sem.at[1]),
        pltpu.make_async_copy(feats.at[0], feats_own, local_sem.at[2]),
        pltpu.make_async_copy(w_qk_in, weights.at[:, pl.ds(0, width)], local_sem.at[3]),
        pltpu.make_async_copy(w_v_in, weights.at[:, pl.ds(width, width)], local_sem.at[4]),
        pltpu.make_async_copy(grad.at[0], grad_own, local_sem.at[5]),
    ]
    for copy in own:
        copy.start()
    pl.semaphore_wait(barrier, me + 1)

    def push(src, dst, send, recv, device):
        return pltpu.make_async_remote_copy(
            src_ref=src, dst_ref=dst, send_sem=send, recv_sem=recv,
            device_id=device, device_id_type=MESH,
        )

    def ship_feats(d, device):
        return push(feats.at[0, mine], feats_in.at[d, mine], f_send.at[d], f_recv.at[d], device)

    def ship_grad(d, device):
        return push(grad.at[0], grad_in.at[d], g_send.at[d], g_recv.at[d], device)

    def ship(d, device):
        ship_feats(d, device).start()
        ship_grad(d, device).start()

    def sent(d, device):
        ship_feats(d, device).wait_send()
        ship_grad(d, device).wait_send()

    def toward(k):
        return {"img": target_of(k)}

    def core(d, half_rows):
        return push(
            feats_in.at[d, half_rows], feats_in.at[d, half_rows], c_send.at[d], c_recv.at[d], partner
        )

    def table_copy(j):
        return push(table.at[me], table.at[me], t_send.at[j], t_recv.at[me], {"img": j})

    def table_wait(j):
        push(table.at[j], table.at[j], t_send.at[j], t_recv.at[j], {"img": j}).wait_recv()

    loop(0, me, lambda j: pl.semaphore_signal(
        ready.at[me], inc=1, device_id={"img": j}, device_id_type=MESH
    ))
    own[0].wait()
    own[1].wait()
    left, right = pair_own[0:1, :], pair_own[1:2, :]
    count_a = jnp.full((1, LANES), count_own[0], jnp.int32)
    table[me] = jnp.concatenate([jnp.full((1, LANES), -1, jnp.int32), count_a], axis=0)
    table[me, 0:1, 0 : pairs.shape[2]] = jnp.where(left >= 0, left * n + right, -1)
    loop(0, me, lambda j: table_copy(j).start())

    targets(1, jnp.minimum(z, reach) + 1, lambda k: ship(k, toward(k)))

    @pl.when(x == 1)
    def _():
        ship(0, across)


    row_ids = lax.broadcasted_iota(jnp.int32, (rows, width), 0)
    sublane_ids = lax.broadcasted_iota(jnp.int32, (rows, rows), 0)
    unit = lax.broadcasted_iota(jnp.int32, (depth, depth), 0) == lax.broadcasted_iota(jnp.int32, (depth, depth), 1)
    unit = jnp.where(unit, 1.0, 0.0).astype(low)

    def stack(part):
        head = lax.broadcasted_iota(jnp.int32, part.shape, 1) // HEAD_DIM
        zero = jnp.zeros((), part.dtype)
        return [jnp.where(head == h, part, zero) for h in range(heads)]

    def project(block, cotangent, count):
        projected = contract(block, weights[...], 1, 0)
        q = projected[:, :width].astype(low)
        g = jnp.where(row_ids < count, cotangent, jnp.zeros((), low))
        turned = contract(turn[...], block, 1, 1).astype(low)
        g_t = contract(unit[:width, :width], g, 1, 1).astype(low)
        return q, projected[:, width:].astype(low), g, turned[:width], g_t, turned[width:]

    def keep(a, block, cotangent, count):
        q, v, g, q_t, g_t, f_t = project(block, cotangent, count)
        part = slice(a * rows, (a + 1) * rows)
        q = (q.astype(jnp.float32) * scale).astype(low)
        q_rows[part], v_rows[part] = q, v
        for h, (q_part, g_part) in enumerate(zip(stack(q), stack(g))):
            spot = slice((2 * h + a) * rows, (2 * h + a + 1) * rows)
            q_heads[spot], g_heads[spot] = q_part, g_part
        q_turned[:, part], g_turned[:, part], feats_turned[:, part] = q_t, g_t, f_t

    for copy in own[2:]:
        copy.wait()

    if n > 1:
        turn[0:width] = contract(unit, weights[:, 0:width], 1, 0).astype(low).T
        turn[width:] = unit
        keep(0, feats_own[...], grad_own[...], count_a)
        total_turned[...] = jnp.zeros_like(total_turned)
        product[...] = jnp.zeros_like(product)

    def greet(j):
        pl.semaphore_wait(ready.at[j], 1)

        @pl.when(j == beside)
        def _():
            ship(0, across)

        k = z - j // 2 + columns

        @pl.when((lax.rem(j, 2) == x) & (k <= span(j // 2)))
        def _():
            ship(k, {"img": j})

        table_copy(j).start()

    loop(me + 1, n, greet)

    def times(a, k):
        image = me if a == 0 else beside
        peer = peer_of(k)
        listed = table[:, 0, :]
        hits = (listed == image * n + peer) | (listed == peer * n + image)
        return jnp.sum(hits.astype(jnp.float32), keepdims=True)

    def side(scores, slope, live):
        masked = jnp.where(live, scores, NEG_FILL)
        e = jnp.exp(masked - jnp.max(masked, axis=0, keepdims=True))
        inverse = 1.0 / jnp.sum(e, axis=0, keepdims=True)
        weighted = slope * e
        mean = jnp.sum(weighted, axis=0, keepdims=True) * inverse
        d = (weighted - e * mean) * (inverse * scale)
        return (e * inverse).astype(low), d.astype(low)

    def weight_copy(j):
        return push(outgoing.at[j], arrived.at[me], w_send.at[j], w_recv.at[me], {"img": j})

    def term_copy(k):
        device = {"img": peer_of(k)}
        return push(term_out.at[k], term_in.at[k], d_send.at[k], d_recv.at[k], device)

    def swap(k):
        return push(swap_out.at[k], swap_in.at[k], s_send.at[k], s_recv.at[k], partner)

    def each_other(body):
        loop(1, n, lambda d: body(lax.rem(me + d, n)))

    def term_of(total):
        return contract(weights[...], total, 1, 0)

    def halve(k, total):
        term = term_of(total)
        for s in range(2):
            term_half[k, s] = term[s * width : (s + 1) * width]
        swap_out[k] = term_half[k, 1 - sub].astype(low)
        swap(k).start()

    def hand_on(k):
        swap(k).wait_recv()
        term_out[k] = (term_half[k, sub] + swap_in[k].astype(jnp.float32)).astype(low)
        term_copy(k).start()

    def slopes_of(k):
        slot = k if held else 0
        peer = peer_of(k)

        @pl.when(k > 0)
        def _():
            ship_feats(k, across).wait_recv()
            core(k, mine).start()
            if held:
                @pl.when(k < end_k - 1)
                def _():
                    table_wait(peer)
            ship_grad(k, across).wait_recv()
            core(k, other).wait_recv()

        count_c = table[peer, 1:2, :]
        count_b = table[beside, 1:2, :]
        block = feats_in[k]
        q, v, g, q_t, g_t, f_t = project(block, grad_in[k], count_c)
        scores = contract(q_rows[...], jnp.concatenate(stack(q), axis=0), 1, 1)
        slopes = contract(v_rows[...], jnp.concatenate(stack(g), axis=0), 1, 1)
        scores_t = contract(q, q_heads[...], 1, 1)
        slopes_t = contract(v, g_heads[...], 1, 1)
        peer_q[slot], peer_g[slot], peer_feats[slot] = q_t, g_t, f_t
        col_live = sublane_ids < count_c
        row_live = [sublane_ids < count_a, sublane_ids < count_b]
        for h in range(heads):
            across_h = slice(h * rows, (h + 1) * rows)
            for a in range(2):
                down = slice(a * rows, (a + 1) * rows)
                cols[slot, down, across_h], dcols[slot, down, across_h] = side(
                    scores[down, across_h], slopes[down, across_h], row_live[a]
                )
                spot = slice((2 * h + a) * rows, (2 * h + a + 1) * rows)
                rows_t[slot, :, spot], drows_t[slot, :, spot] = side(
                    scores_t[:, spot], slopes_t[:, spot], col_live
                )

    def gather_grads(k, final):
        slot = k if held else 0
        factor = jnp.concatenate(
            [jnp.broadcast_to(times(a, k), (1, rows)) for a in range(2)], axis=1
        )
        x_q, x_v, y_q, y_v = [], [], [], []
        for h in range(heads):
            head = slice(h * HEAD_DIM, (h + 1) * HEAD_DIM)
            across_h, spot = slice(h * rows, (h + 1) * rows), slice(2 * h * rows, 2 * (h + 1) * rows)
            col, dcol = cols[slot, :, across_h], dcols[slot, :, across_h]
            row_t, drow_t = rows_t[slot, :, spot], drows_t[slot, :, spot]
            q_a = (q_turned[head].astype(jnp.float32) * factor).astype(low)
            g_a = (g_turned[head].astype(jnp.float32) * factor).astype(low)
            q_c, g_c = peer_q[slot, head], peer_g[slot, head]
            x_q.append(contract(q_c, dcol, 1, 1) + contract(q_c, drow_t, 1, 0))
            x_v.append(contract(g_c, col, 1, 1))
            y_q.append(contract(q_a, dcol, 1, 0) + contract(q_a, drow_t, 1, 1))
            y_v.append(contract(g_a, row_t, 1, 1))
        x_t = jnp.concatenate(x_q + x_v, axis=0) * factor
        y_t = jnp.concatenate(y_q + y_v, axis=0)
        y_low = y_t.astype(low)

        @pl.when(k > 0)
        def _():
            halve(k, y_low)

        weight_term = contract(feats_turned[...], x_t.astype(low), 1, 1)
        weight_term = product[...] + weight_term + contract(peer_feats[slot], y_low, 1, 1)
        if final:
            for c in range(n):
                piece = weight_term[c * share : (c + 1) * share]
                terms[c] = piece
                outgoing[c] = piece.astype(low)
            each_other(lambda j: weight_copy(j).start())
        else:
            product[...] = weight_term
        total_turned[...] += x_t

        @pl.when(k == 0)
        def _():
            total_turned[:, rows:] += y_t

    if n > 1:
        ship_feats(0, across).wait_recv()
        core(0, mine).start()
        table_wait(beside)
        ship_grad(0, across).wait_recv()
        core(0, other).wait_recv()
        keep(1, feats_in[0], grad_in[0], table[beside, 1:2, :])

        def every_table():
            def one(d):
                column = lax.rem(z + d, columns)
                table_wait(column * 2 + 1 - x)
                known = (d < end_k - 1) if held else False

                @pl.when(jnp.logical_not(known))
                def _():
                    table_wait(column * 2 + x)

            loop(1, columns, one)

        if held:
            loop(first_k, end_k - 1, slopes_of)
            every_table()
            loop(first_k, end_k - 1, lambda k: gather_grads(k, False))
            loop(1, end_k - 1, hand_on)
        else:
            every_table()

            def step(k):
                slopes_of(k)
                gather_grads(k, False)

                @pl.when(k > 0)
                def _():
                    hand_on(k)

            loop(first_k, end_k - 1, step)
        slopes_of(end_k - 1)
        gather_grads(end_k - 1, True)

        @pl.when(end_k > 1)
        def _():
            hand_on(end_k - 1)

        halve(0, total_turned[:, rows:].astype(low))
        halve(columns, total_turned[:, :rows].astype(low))
        hand_on(0)
        swap(columns).wait_recv()
        term_own[...] = term_half[columns, sub] + swap_in[columns].astype(jnp.float32)

    def take(k):
        push(term_out.at[k], term_in.at[k], d_send.at[k], d_recv.at[k], across).wait_recv()
        term_own[...] += term_in[k].astype(jnp.float32)

    take(0)
    targets(1, reach + 1, take)
    grad_feats[0] = term_own[...].T.astype(grad_feats.dtype)

    def weight_wait(j):
        push(outgoing.at[j], arrived.at[j], w_send.at[j], w_recv.at[j], across).wait_recv()

    each_other(weight_wait)
    total = terms[me]
    for d in range(1, n):
        total = total + arrived[lax.rem(me + d, n)].astype(jnp.float32)
    grad_weights[0] = total[:, :width]
    grad_weights[1] = total[:, width:]

    targets(1, reach + 1, lambda k: sent(k, toward(k)))
    sent(0, across)
    if n > 1:
        each_other(lambda j: table_copy(j).wait_send())
        loop(0, end_k, lambda k: core(k, mine).wait_send())
        each_other(lambda j: weight_copy(j).wait_send())
        loop(0, end_k, lambda k: swap(k).wait_send())
        swap(columns).wait_send()
        loop(0, end_k, lambda k: term_copy(k).wait_send())


def store(feats_from, weights_from, feats_to, weights_to, sem):
    copies = [
        pltpu.make_async_copy(feats_from, feats_to, sem.at[0]),
        pltpu.make_async_copy(weights_from, weights_to, sem.at[1]),
    ]
    for copy in copies:
        copy.start()
    for copy in copies:
        copy.wait()


def local(feats, grad_msg, w_qk, w_v, pair_slots, counts):
    n = lax.axis_size("img")
    columns = n // 2
    held = columns if columns <= HELD_COLUMNS else 1
    rows, depth = feats.shape[1:]
    width = w_qk.shape[1]
    heads = width // HEAD_DIM
    share = depth // n
    slots = pair_slots.shape[1]
    low, full = jnp.bfloat16, jnp.float32
    vmem = pltpu.VMEM
    dma = pltpu.SemaphoreType.DMA
    results = pl.pallas_call(
        functools.partial(kernel, n),
        out_shape=(
            vmem((1, rows, width), low),
            vmem((2, share, width), full),
        ),
        in_specs=[HBM] * 6,
        out_specs=(VMEM,) * 2,
        scratch_shapes=[
            vmem((rows, depth), low),
            vmem((rows, width), low),
            vmem((columns, rows, depth), low),
            vmem((columns, rows, width), low),
            vmem((2, slots), jnp.int32),
            pltpu.SMEM((1,), jnp.int32),
            vmem((n, 2, LANES), jnp.int32),
            vmem((depth, 2 * width), low),
            vmem((width + depth, depth), low),
            vmem((2 * rows, width), low),
            vmem((2 * rows, width), low),
            vmem((2 * heads * rows, width), low),
            vmem((2 * heads * rows, width), low),
            vmem((width, 2 * rows), low),
            vmem((width, 2 * rows), low),
            vmem((depth, 2 * rows), low),
            vmem((2 * width, 2 * rows), full),
            vmem((depth, 2 * width), full),
            vmem((held, 2 * rows, heads * rows), low),
            vmem((held, 2 * rows, heads * rows), low),
            vmem((held, rows, 2 * heads * rows), low),
            vmem((held, rows, 2 * heads * rows), low),
            vmem((held, width, rows), low),
            vmem((held, width, rows), low),
            vmem((held, depth, rows), low),
            vmem((n, share, 2 * width), full),
            vmem((n, share, 2 * width), low),
            vmem((n, share, 2 * width), low),
            vmem((width, rows), full),
            vmem((columns + 1, 2, width, rows), full),
            vmem((columns, width, rows), low),
            vmem((columns, width, rows), low),
            vmem((columns + 1, width, rows), low),
            vmem((columns + 1, width, rows), low),
            dma((6,)), pltpu.SemaphoreType.REGULAR((n,)),
            dma((columns,)), dma((columns,)), dma((columns,)),
            dma((columns,)), dma((columns,)), dma((columns,)),
            dma((n,)), dma((n,)), dma((n,)), dma((n,)),
            dma((columns,)), dma((columns,)), dma((columns + 1,)), dma((columns + 1,)),
        ],
        compiler_params=pltpu.CompilerParams(
            collective_id=0, has_side_effects=True, vmem_limit_bytes=60 * 1024 * 1024
        ),
        name="backward",
    )(feats, grad_msg, w_qk, w_v, jnp.transpose(pair_slots, (0, 2, 1)), counts)
    any_space = pl.BlockSpec(memory_space=pltpu.VMEM)
    return pl.pallas_call(
        store,
        out_shape=(
            jax.ShapeDtypeStruct((1, rows, width), low),
            jax.ShapeDtypeStruct((2, share, width), full),
        ),
        in_specs=[any_space] * 2,
        out_specs=(pl.BlockSpec(memory_space=pl.ANY),) * 2,
        scratch_shapes=[dma((2,))],
        name="store",
    )(*(pltpu.with_memory_space_constraint(result, pltpu.VMEM) for result in results))


def solution(mesh):
    in_specs = (
        P(("groups", "img"), None, None),
        P(("groups", "img"), None, "sub"),
        P(None, "sub"),
        P(None, "sub"),
        P(("groups", "img"), None, None),
        P(("groups", "img")),
    )
    out_specs = (P(("groups", "img"), None, "sub"), P("groups", "img", "sub"))
    return jax.shard_map(local, mesh=mesh, in_specs=in_specs, out_specs=out_specs, check_vma=False)
```

```python
import functools

import jax
import jax.numpy as jnp
from jax import lax
from jax.experimental import pallas as pl
from jax.experimental.pallas import tpu as pltpu
from jax.sharding import PartitionSpec as P

HEAD_DIM = 64
NEG_FILL = -1e30
LANES = 128
HELD_COLUMNS = 8
MESH = pl.DeviceIdType.MESH
HBM = pl.BlockSpec(memory_space=pltpu.HBM)
VMEM = pl.BlockSpec(memory_space=pltpu.VMEM)


def contract(left, right, left_dim, right_dim):
    return lax.dot_general(
        left, right, (((left_dim,), (right_dim,)), ((), ())), preferred_element_type=jnp.float32
    )


def loop(low, high, body):
    def step(d, carry):
        body(d)
        return carry

    lax.fori_loop(low, high, step, 0)


def static_loop(low, high, body):
    if high - low <= 8:
        for d in range(low, high):
            body(d)
    else:
        loop(low, high, body)


def kernel(
    n, feats, grad, w_qk_in, w_v_in, pairs, counts, grad_feats, grad_weights,
    feats_own, grad_own, feats_in, grad_in, pair_own, count_own, table, weights,
    turn, q_rows, v_rows, q_heads, g_heads, q_turned, g_turned, feats_turned, total_turned, product,
    cols, dcols, rows_t, drows_t, peer_q, peer_g, peer_feats,
    terms, outgoing, arrived, term_own, last_out, last_in, term_half, term_out, term_in, swap_out, swap_in,
    local_sem, ready, f_send, g_send, c_send, f_recv, g_recv, c_recv, t_send, t_recv,
    w_send, w_recv, d_send, d_recv, s_send, s_recv, l_send, l_recv,
):
    me = lax.axis_index("img")
    sub = lax.axis_index("sub")
    columns = n // 2
    held = columns <= HELD_COLUMNS
    z, x = me // 2, lax.rem(me, 2)
    rows = feats.shape[1]
    half = rows // 2
    width = w_qk_in.shape[1]
    heads = width // HEAD_DIM
    scale = HEAD_DIM ** (-0.5)
    share = terms.shape[1]
    depth = feats.shape[2]
    low = jnp.bfloat16
    mine = pl.ds(pl.multiple_of(sub * half, half), half)
    other = pl.ds(pl.multiple_of((1 - sub) * half, half), half)
    beside = me + 1 - 2 * x
    across = {"img": beside}
    partner = {"sub": 1 - sub}
    reach = columns // 2

    def span(column):
        return reach - 1 + jnp.where(column < reach, 1, 0)

    def peer_of(k):
        return jnp.where(k == 0, beside, lax.rem(z + k, columns) * 2 + x)

    def target_of(k):
        return lax.rem(z - k + columns, columns) * 2 + x

    def targets(low_k, high_k, body):
        def one(k):
            @pl.when(k <= span(lax.rem(z - k + columns, columns)))
            def _():
                body(k)

        loop(low_k, high_k, one)

    first_k, end_k = x, span(z) + 1

    barrier = pltpu.get_barrier_semaphore()
    pl.semaphore_signal(barrier, inc=1, device_id=partner, device_id_type=MESH)
    loop(me + 1, n, lambda j: pl.semaphore_signal(
        barrier, inc=1, device_id={"img": j}, device_id_type=MESH
    ))
    own = [
        pltpu.make_async_copy(pairs.at[0], pair_own, local_sem.at[0]),
        pltpu.make_async_copy(counts, count_own, local_sem.at[1]),
        pltpu.make_async_copy(feats.at[0], feats_own, local_sem.at[2]),
        pltpu.make_async_copy(grad.at[0], grad_own, local_sem.at[5]),
        pltpu.make_async_copy(w_qk_in, weights.at[:, pl.ds(0, width)], local_sem.at[3]),
        pltpu.make_async_copy(w_v_in, weights.at[:, pl.ds(width, width)], local_sem.at[4]),
    ]
    for copy in own:
        copy.start()
    pl.semaphore_wait(barrier, me + 1)

    def push(src, dst, send, recv, device):
        return pltpu.make_async_remote_copy(
            src_ref=src, dst_ref=dst, send_sem=send, recv_sem=recv,
            device_id=device, device_id_type=MESH,
        )

    def ship_feats(d, device):
        return push(feats_own.at[mine], feats_in.at[d, mine], f_send.at[d], f_recv.at[d], device)

    def ship_grad(d, device):
        return push(grad_own, grad_in.at[d], g_send.at[d], g_recv.at[d], device)

    def ship(d, device):
        ship_feats(d, device).start()
        ship_grad(d, device).start()

    def sent(d, device):
        ship_feats(d, device).wait_send()
        ship_grad(d, device).wait_send()

    def toward(k):
        return {"img": target_of(k)}

    def core(d, half_rows):
        return push(
            feats_in.at[d, half_rows], feats_in.at[d, half_rows], c_send.at[d], c_recv.at[d], partner
        )

    def table_copy(j):
        return push(table.at[me], table.at[me], t_send.at[j], t_recv.at[me], {"img": j})

    def table_wait(j):
        push(table.at[j], table.at[j], t_send.at[j], t_recv.at[j], {"img": j}).wait_recv()

    loop(0, me, lambda j: pl.semaphore_signal(
        ready.at[me], inc=1, device_id={"img": j}, device_id_type=MESH
    ))
    own[0].wait()
    own[1].wait()
    left, right = pair_own[0:1, :], pair_own[1:2, :]
    count_a = jnp.full((1, LANES), count_own[0], jnp.int32)
    table[me] = jnp.concatenate([jnp.full((1, LANES), -1, jnp.int32), count_a], axis=0)
    table[me, 0:1, 0 : pairs.shape[2]] = jnp.where(left >= 0, left * n + right, -1)
    loop(0, me, lambda j: table_copy(j).start())

    own[2].wait()
    own[3].wait()
    targets(1, jnp.minimum(z, reach) + 1, lambda k: ship(k, toward(k)))

    @pl.when(x == 1)
    def _():
        ship(0, across)


    row_ids = lax.broadcasted_iota(jnp.int32, (rows, width), 0)
    sublane_ids = lax.broadcasted_iota(jnp.int32, (rows, rows), 0)
    unit = lax.broadcasted_iota(jnp.int32, (depth, depth), 0) == lax.broadcasted_iota(jnp.int32, (depth, depth), 1)
    unit = jnp.where(unit, 1.0, 0.0).astype(low)

    def stack(part):
        head = lax.broadcasted_iota(jnp.int32, part.shape, 1) // HEAD_DIM
        zero = jnp.zeros((), part.dtype)
        return [jnp.where(head == h, part, zero) for h in range(heads)]

    def project(block, cotangent, count):
        projected = contract(block, weights[...], 1, 0)
        q = projected[:, :width].astype(low)
        g = jnp.where(row_ids < count, cotangent, jnp.zeros((), low))
        turned = contract(turn[...], block, 1, 1).astype(low)
        g_t = contract(unit[:width, :width], g, 1, 1).astype(low)
        return q, projected[:, width:].astype(low), g, turned[:width], g_t, turned[width:]

    def keep(a, block, cotangent, count):
        q, v, g, q_t, g_t, f_t = project(block, cotangent, count)
        part = slice(a * rows, (a + 1) * rows)
        q = (q.astype(jnp.float32) * scale).astype(low)
        q_rows[part], v_rows[part] = q, v
        for h, (q_part, g_part) in enumerate(zip(stack(q), stack(g))):
            spot = slice((2 * h + a) * rows, (2 * h + a + 1) * rows)
            q_heads[spot], g_heads[spot] = q_part, g_part
        q_turned[:, part], g_turned[:, part], feats_turned[:, part] = q_t, g_t, f_t

    for copy in own[4:]:
        copy.wait()

    if n > 1:
        turn[0:width] = contract(unit, weights[:, 0:width], 1, 0).astype(low).T
        turn[width:] = unit
        keep(0, feats_own[...], grad_own[...], count_a)
        total_turned[...] = jnp.zeros_like(total_turned)
        product[...] = jnp.zeros_like(product)

    def greet(j):
        pl.semaphore_wait(ready.at[j], 1)

        @pl.when(j == beside)
        def _():
            ship(0, across)

        k = z - j // 2 + columns

        @pl.when((lax.rem(j, 2) == x) & (k <= span(j // 2)))
        def _():
            ship(k, {"img": j})

        table_copy(j).start()

    loop(me + 1, n, greet)

    def times(a, k):
        image = me if a == 0 else beside
        peer = peer_of(k)
        listed = table[:, 0, :]
        hits = (listed == image * n + peer) | (listed == peer * n + image)
        return jnp.sum(hits.astype(jnp.float32), keepdims=True)

    def side(scores, slope, live):
        masked = jnp.where(live, scores, NEG_FILL)
        e = jnp.exp(masked - jnp.max(masked, axis=0, keepdims=True))
        inverse = 1.0 / jnp.sum(e, axis=0, keepdims=True)
        weighted = slope * e
        mean = jnp.sum(weighted, axis=0, keepdims=True) * inverse
        d = (weighted - e * mean) * (inverse * scale)
        return (e * inverse).astype(low), d.astype(low)

    def weight_copy(j):
        return push(outgoing.at[j], arrived.at[me], w_send.at[j], w_recv.at[me], {"img": j})

    def term_copy(k):
        device = {"img": peer_of(k)}
        return push(term_out.at[k], term_in.at[k], d_send.at[k], d_recv.at[k], device)

    def last_copy(k, s):
        device = {"img": peer_of(k), "sub": s}
        return push(last_out.at[s], last_in.at[sub], l_send.at[s], l_recv.at[sub], device)

    def swap(k):
        return push(swap_out.at[k], swap_in.at[k], s_send.at[k], s_recv.at[k], partner)

    def each_other(body):
        loop(1, n, lambda d: body(lax.rem(me + d, n)))

    def term_of(total):
        return contract(weights[...], total, 1, 0)

    def halve(k, total):
        term = term_of(total)
        for s in range(2):
            term_half[k, s] = term[s * width : (s + 1) * width]
        swap_out[k] = term_half[k, 1 - sub].astype(low)
        swap(k).start()

    def hand_on(k):
        swap(k).wait_recv()
        term_out[k] = (term_half[k, sub] + swap_in[k].astype(jnp.float32)).astype(low)
        term_copy(k).start()

    def slopes_of(k):
        slot = k if held else 0
        peer = peer_of(k)

        @pl.when(k > 0)
        def _():
            ship_feats(k, across).wait_recv()
            core(k, mine).start()
            if held:
                @pl.when(k < end_k - 1)
                def _():
                    table_wait(peer)
            ship_grad(k, across).wait_recv()
            core(k, other).wait_recv()

        count_c = table[peer, 1:2, :]
        count_b = table[beside, 1:2, :]
        block = feats_in[k]
        q, v, g, q_t, g_t, f_t = project(block, grad_in[k], count_c)
        scores = contract(q_rows[...], jnp.concatenate(stack(q), axis=0), 1, 1)
        slopes = contract(v_rows[...], jnp.concatenate(stack(g), axis=0), 1, 1)
        scores_t = contract(q, q_heads[...], 1, 1)
        slopes_t = contract(v, g_heads[...], 1, 1)
        peer_q[slot], peer_g[slot], peer_feats[slot] = q_t, g_t, f_t
        col_live = sublane_ids < count_c
        row_live = [sublane_ids < count_a, sublane_ids < count_b]
        for h in range(heads):
            across_h = slice(h * rows, (h + 1) * rows)
            for a in range(2):
                down = slice(a * rows, (a + 1) * rows)
                cols[slot, down, across_h], dcols[slot, down, across_h] = side(
                    scores[down, across_h], slopes[down, across_h], row_live[a]
                )
                spot = slice((2 * h + a) * rows, (2 * h + a + 1) * rows)
                rows_t[slot, :, spot], drows_t[slot, :, spot] = side(
                    scores_t[:, spot], slopes_t[:, spot], col_live
                )

    def gather_grads(k, final):
        slot = k if held else 0
        factor = jnp.concatenate(
            [jnp.broadcast_to(times(a, k), (1, rows)) for a in range(2)], axis=1
        )
        x_q, x_v, y_q, y_v = [], [], [], []
        for h in range(heads):
            head = slice(h * HEAD_DIM, (h + 1) * HEAD_DIM)
            across_h, spot = slice(h * rows, (h + 1) * rows), slice(2 * h * rows, 2 * (h + 1) * rows)
            col, dcol = cols[slot, :, across_h], dcols[slot, :, across_h]
            row_t, drow_t = rows_t[slot, :, spot], drows_t[slot, :, spot]
            q_a = (q_turned[head].astype(jnp.float32) * factor).astype(low)
            g_a = (g_turned[head].astype(jnp.float32) * factor).astype(low)
            q_c, g_c = peer_q[slot, head], peer_g[slot, head]
            x_q.append(contract(q_c, dcol, 1, 1) + contract(q_c, drow_t, 1, 0))
            x_v.append(contract(g_c, col, 1, 1))
            y_q.append(contract(q_a, dcol, 1, 0) + contract(q_a, drow_t, 1, 1))
            y_v.append(contract(g_a, row_t, 1, 1))
        x_t = jnp.concatenate(x_q + x_v, axis=0) * factor
        y_t = jnp.concatenate(y_q + y_v, axis=0)
        y_low = y_t.astype(low)

        round_it = final & (z + k >= columns)

        @pl.when(round_it)
        def _():
            term = term_of(y_low)
            for s in range(2):
                last_out[s] = term[s * width : (s + 1) * width].astype(low)
                last_copy(k, s).start()

        @pl.when((k > 0) & jnp.logical_not(round_it))
        def _():
            halve(k, y_low)

        weight_term = contract(feats_turned[...], x_t.astype(low), 1, 1)
        weight_term = product[...] + weight_term + contract(peer_feats[slot], y_low, 1, 1)
        if final:
            for c in range(n):
                piece = weight_term[c * share : (c + 1) * share]
                terms[c] = piece
                outgoing[c] = piece.astype(low)
            loop(0, me, lambda j: weight_copy(j).start())
            loop(me + 1, n, lambda j: weight_copy(j).start())
        else:
            product[...] = weight_term
        total_turned[...] += x_t

        @pl.when(k == 0)
        def _():
            total_turned[:, rows:] += y_t

    if n > 1:
        ship_feats(0, across).wait_recv()
        core(0, mine).start()
        table_wait(beside)
        ship_grad(0, across).wait_recv()
        core(0, other).wait_recv()
        keep(1, feats_in[0], grad_in[0], table[beside, 1:2, :])

        def every_table():
            def one(d):
                column = lax.rem(z + d, columns)
                table_wait(column * 2 + 1 - x)
                known = (d < end_k - 1) if held else False

                @pl.when(jnp.logical_not(known))
                def _():
                    table_wait(column * 2 + x)

            loop(1, columns, one)

        if held:
            loop(first_k, end_k - 1, slopes_of)
            every_table()
            loop(first_k, end_k - 1, lambda k: gather_grads(k, False))
        else:
            every_table()

            def step(k):
                slopes_of(k)
                gather_grads(k, False)

                @pl.when(k > 0)
                def _():
                    hand_on(k)

            loop(first_k, end_k - 1, step)
        slopes_of(end_k - 1)
        if held:
            loop(1, end_k - 1, hand_on)
        gather_grads(end_k - 1, True)

        @pl.when(z + end_k <= columns)
        def _():
            hand_on(end_k - 1)

        halve(0, total_turned[:, rows:].astype(low))
        halve(columns, total_turned[:, :rows].astype(low))
        hand_on(0)
        swap(columns).wait_recv()
        term_own[...] = term_half[columns, sub] + swap_in[columns].astype(jnp.float32)

    def weight_wait(j):
        push(outgoing.at[j], arrived.at[j], w_send.at[j], w_recv.at[j], across).wait_recv()

    each_other(weight_wait)
    total = terms[me]
    for d in range(1, n):
        total = total + arrived[lax.rem(me + d, n)].astype(jnp.float32)
    grad_weights[0] = total[:, :width]
    grad_weights[1] = total[:, width:]

    targets(1, reach + 1, lambda k: sent(k, toward(k)))
    sent(0, across)
    if n > 1:
        each_other(lambda j: table_copy(j).wait_send())
        loop(0, end_k, lambda k: core(k, mine).wait_send())
        each_other(lambda j: weight_copy(j).wait_send())
        swapped = jnp.where(z + end_k > columns, end_k - 1, end_k)
        loop(0, swapped, lambda k: swap(k).wait_send())
        swap(columns).wait_send()
        loop(0, swapped, lambda k: term_copy(k).wait_send())

        @pl.when(z + end_k > columns)
        def _():
            for s in range(2):
                last_copy(end_k - 1, s).wait_send()

    def take(k):
        push(term_out.at[k], term_in.at[k], d_send.at[k], d_recv.at[k], across).wait_recv()
        term_own[...] += term_in[k].astype(jnp.float32)

    def take_either(k):
        sender = lax.rem(z - k + columns, columns)
        ends = (k > z) & (k == span(sender))

        @pl.when(ends)
        def _():
            for s in range(2):
                push(last_out.at[s], last_in.at[s], l_send.at[s], l_recv.at[s], across).wait_recv()
            term_own[...] += last_in[0].astype(jnp.float32) + last_in[1].astype(jnp.float32)

        @pl.when(jnp.logical_not(ends))
        def _():
            take(k)

    take(0)
    targets(1, reach + 1, take_either)
    grad_feats[0] = term_own[...].T.astype(grad_feats.dtype)


def store(feats_from, weights_from, feats_to, weights_to, sem):
    copies = [
        pltpu.make_async_copy(feats_from, feats_to, sem.at[0]),
        pltpu.make_async_copy(weights_from, weights_to, sem.at[1]),
    ]
    for copy in copies:
        copy.start()
    for copy in copies:
        copy.wait()


def local(feats, grad_msg, w_qk, w_v, pair_slots, counts):
    n = lax.axis_size("img")
    columns = n // 2
    held = columns if columns <= HELD_COLUMNS else 1
    rows, depth = feats.shape[1:]
    width = w_qk.shape[1]
    heads = width // HEAD_DIM
    share = depth // n
    slots = pair_slots.shape[1]
    low, full = jnp.bfloat16, jnp.float32
    vmem = pltpu.VMEM
    dma = pltpu.SemaphoreType.DMA
    results = pl.pallas_call(
        functools.partial(kernel, n),
        out_shape=(
            vmem((1, rows, width), low),
            vmem((2, share, width), full),
        ),
        in_specs=[HBM] * 6,
        out_specs=(VMEM,) * 2,
        scratch_shapes=[
            vmem((rows, depth), low),
            vmem((rows, width), low),
            vmem((columns, rows, depth), low),
            vmem((columns, rows, width), low),
            vmem((2, slots), jnp.int32),
            pltpu.SMEM((1,), jnp.int32),
            vmem((n, 2, LANES), jnp.int32),
            vmem((depth, 2 * width), low),
            vmem((width + depth, depth), low),
            vmem((2 * rows, width), low),
            vmem((2 * rows, width), low),
            vmem((2 * heads * rows, width), low),
            vmem((2 * heads * rows, width), low),
            vmem((width, 2 * rows), low),
            vmem((width, 2 * rows), low),
            vmem((depth, 2 * rows), low),
            vmem((2 * width, 2 * rows), full),
            vmem((depth, 2 * width), full),
            vmem((held, 2 * rows, heads * rows), low),
            vmem((held, 2 * rows, heads * rows), low),
            vmem((held, rows, 2 * heads * rows), low),
            vmem((held, rows, 2 * heads * rows), low),
            vmem((held, width, rows), low),
            vmem((held, width, rows), low),
            vmem((held, depth, rows), low),
            vmem((n, share, 2 * width), full),
            vmem((n, share, 2 * width), low),
            vmem((n, share, 2 * width), low),
            vmem((width, rows), full),
            vmem((2, width, rows), low),
            vmem((2, width, rows), low),
            vmem((columns + 1, 2, width, rows), full),
            vmem((columns, width, rows), low),
            vmem((columns, width, rows), low),
            vmem((columns + 1, width, rows), low),
            vmem((columns + 1, width, rows), low),
            dma((6,)), pltpu.SemaphoreType.REGULAR((n,)),
            dma((columns,)), dma((columns,)), dma((columns,)),
            dma((columns,)), dma((columns,)), dma((columns,)),
            dma((n,)), dma((n,)), dma((n,)), dma((n,)),
            dma((columns,)), dma((columns,)), dma((columns + 1,)), dma((columns + 1,)),
            dma((2,)), dma((2,)),
        ],
        compiler_params=pltpu.CompilerParams(
            collective_id=0, has_side_effects=True, vmem_limit_bytes=60 * 1024 * 1024
        ),
        name="backward",
    )(feats, grad_msg, w_qk, w_v, jnp.transpose(pair_slots, (0, 2, 1)), counts)
    any_space = pl.BlockSpec(memory_space=pltpu.VMEM)
    return pl.pallas_call(
        store,
        out_shape=(
            jax.ShapeDtypeStruct((1, rows, width), low),
            jax.ShapeDtypeStruct((2, share, width), full),
        ),
        in_specs=[any_space] * 2,
        out_specs=(pl.BlockSpec(memory_space=pl.ANY),) * 2,
        scratch_shapes=[dma((2,))],
        name="store",
    )(*(pltpu.with_memory_space_constraint(result, pltpu.VMEM) for result in results))


def solution(mesh):
    in_specs = (
        P(("groups", "img"), None, None),
        P(("groups", "img"), None, "sub"),
        P(None, "sub"),
        P(None, "sub"),
        P(("groups", "img"), None, None),
        P(("groups", "img")),
    )
    out_specs = (P(("groups", "img"), None, "sub"), P("groups", "img", "sub"))
    return jax.shard_map(local, mesh=mesh, in_specs=in_specs, out_specs=out_specs, check_vma=False)
```

```python
import functools

import jax
import jax.numpy as jnp
from jax import lax
from jax.experimental import pallas as pl
from jax.experimental.pallas import tpu as pltpu
from jax.sharding import PartitionSpec as P

HEAD_DIM = 64
NEG_FILL = -1e30
LANES = 128
HELD_COLUMNS = 8
MESH = pl.DeviceIdType.MESH
HBM = pl.BlockSpec(memory_space=pltpu.HBM)
VMEM = pl.BlockSpec(memory_space=pltpu.VMEM)


def contract(left, right, left_dim, right_dim):
    return lax.dot_general(
        left, right, (((left_dim,), (right_dim,)), ((), ())), preferred_element_type=jnp.float32
    )


def loop(low, high, body):
    def step(d, carry):
        body(d)
        return carry

    lax.fori_loop(low, high, step, 0)


def static_loop(low, high, body):
    if high - low <= 8:
        for d in range(low, high):
            body(d)
    else:
        loop(low, high, body)


def kernel(
    n, feats, grad, w_qk_in, w_v_in, pairs, counts, grad_feats, grad_weights,
    feats_own, grad_own, feats_in, grad_in, pair_own, count_own, table, weights,
    turn, q_rows, v_rows, q_heads, g_heads, q_turned, g_turned, feats_turned, total_turned, product,
    cols, dcols, rows_t, drows_t, peer_q, peer_g, peer_feats,
    terms, outgoing, arrived, term_own, last_out, last_in, term_half, term_out, term_in, swap_out, swap_in,
    local_sem, ready, f_send, g_send, c_send, f_recv, g_recv, c_recv, t_send, t_recv,
    w_send, w_recv, d_send, d_recv, s_send, s_recv, l_send, l_recv,
):
    me = lax.axis_index("img")
    sub = lax.axis_index("sub")
    columns = n // 2
    held = columns <= HELD_COLUMNS
    z, x = me // 2, lax.rem(me, 2)
    rows = feats.shape[1]
    half = rows // 2
    width = w_qk_in.shape[1]
    heads = width // HEAD_DIM
    scale = HEAD_DIM ** (-0.5)
    share = terms.shape[1]
    depth = feats.shape[2]
    low = jnp.bfloat16
    mine = pl.ds(pl.multiple_of(sub * half, half), half)
    other = pl.ds(pl.multiple_of((1 - sub) * half, half), half)
    beside = me + 1 - 2 * x
    across = {"img": beside}
    partner = {"sub": 1 - sub}
    reach = columns // 2

    def span(column):
        return reach - 1 + jnp.where(column < reach, 1, 0)

    def peer_of(k):
        return jnp.where(k == 0, beside, lax.rem(z + k, columns) * 2 + x)

    def target_of(k):
        return lax.rem(z - k + columns, columns) * 2 + x

    def targets(low_k, high_k, body):
        def one(k):
            @pl.when(k <= span(lax.rem(z - k + columns, columns)))
            def _():
                body(k)

        loop(low_k, high_k, one)

    first_k, end_k = x, span(z) + 1

    barrier = pltpu.get_barrier_semaphore()
    pl.semaphore_signal(barrier, inc=1, device_id=partner, device_id_type=MESH)
    loop(me + 1, n, lambda j: pl.semaphore_signal(
        barrier, inc=1, device_id={"img": j}, device_id_type=MESH
    ))
    own = [
        pltpu.make_async_copy(pairs.at[0], pair_own, local_sem.at[0]),
        pltpu.make_async_copy(counts, count_own, local_sem.at[1]),
        pltpu.make_async_copy(feats.at[0], feats_own, local_sem.at[2]),
        pltpu.make_async_copy(grad.at[0], grad_own, local_sem.at[5]),
        pltpu.make_async_copy(w_qk_in, weights.at[:, pl.ds(0, width)], local_sem.at[3]),
        pltpu.make_async_copy(w_v_in, weights.at[:, pl.ds(width, width)], local_sem.at[4]),
    ]
    for copy in own:
        copy.start()
    pl.semaphore_wait(barrier, me + 1)

    def push(src, dst, send, recv, device):
        return pltpu.make_async_remote_copy(
            src_ref=src, dst_ref=dst, send_sem=send, recv_sem=recv,
            device_id=device, device_id_type=MESH,
        )

    def ship_feats(d, device):
        return push(feats_own.at[mine], feats_in.at[d, mine], f_send.at[d], f_recv.at[d], device)

    def ship_grad(d, device):
        return push(grad_own, grad_in.at[d], g_send.at[d], g_recv.at[d], device)

    def ship(d, device):
        ship_feats(d, device).start()
        ship_grad(d, device).start()

    def sent(d, device):
        ship_feats(d, device).wait_send()
        ship_grad(d, device).wait_send()

    def toward(k):
        return {"img": target_of(k)}

    def core(d, half_rows):
        return push(
            feats_in.at[d, half_rows], feats_in.at[d, half_rows], c_send.at[d], c_recv.at[d], partner
        )

    def table_copy(j):
        return push(table.at[me], table.at[me], t_send.at[j], t_recv.at[me], {"img": j})

    def table_wait(j):
        push(table.at[j], table.at[j], t_send.at[j], t_recv.at[j], {"img": j}).wait_recv()

    loop(0, me, lambda j: pl.semaphore_signal(
        ready.at[me], inc=1, device_id={"img": j}, device_id_type=MESH
    ))
    own[0].wait()
    own[1].wait()
    left, right = pair_own[0:1, :], pair_own[1:2, :]
    count_a = jnp.full((1, LANES), count_own[0], jnp.int32)
    table[me] = jnp.concatenate([jnp.full((1, LANES), -1, jnp.int32), count_a], axis=0)
    table[me, 0:1, 0 : pairs.shape[2]] = jnp.where(left >= 0, left * n + right, -1)
    loop(0, me, lambda j: table_copy(j).start())

    own[2].wait()
    own[3].wait()
    targets(1, jnp.minimum(z, reach) + 1, lambda k: ship(k, toward(k)))

    @pl.when(x == 1)
    def _():
        ship(0, across)


    row_ids = lax.broadcasted_iota(jnp.int32, (rows, width), 0)
    sublane_ids = lax.broadcasted_iota(jnp.int32, (rows, rows), 0)
    unit = lax.broadcasted_iota(jnp.int32, (depth, depth), 0) == lax.broadcasted_iota(jnp.int32, (depth, depth), 1)
    unit = jnp.where(unit, 1.0, 0.0).astype(low)

    def stack(part):
        head = lax.broadcasted_iota(jnp.int32, part.shape, 1) // HEAD_DIM
        zero = jnp.zeros((), part.dtype)
        return [jnp.where(head == h, part, zero) for h in range(heads)]

    def project(block, cotangent, count):
        projected = contract(block, weights[...], 1, 0)
        q = projected[:, :width].astype(low)
        g = jnp.where(row_ids < count, cotangent, jnp.zeros((), low))
        turned = contract(turn[...], block, 1, 1).astype(low)
        g_t = contract(unit[:width, :width], g, 1, 1).astype(low)
        return q, projected[:, width:].astype(low), g, turned[:width], g_t, turned[width:]

    def keep(a, block, cotangent, count):
        q, v, g, q_t, g_t, f_t = project(block, cotangent, count)
        part = slice(a * rows, (a + 1) * rows)
        q = (q.astype(jnp.float32) * scale).astype(low)
        q_rows[part], v_rows[part] = q, v
        for h, (q_part, g_part) in enumerate(zip(stack(q), stack(g))):
            spot = slice((2 * h + a) * rows, (2 * h + a + 1) * rows)
            q_heads[spot], g_heads[spot] = q_part, g_part
        q_turned[:, part], g_turned[:, part], feats_turned[:, part] = q_t, g_t, f_t

    for copy in own[4:]:
        copy.wait()

    if n > 1:
        turn[0:width] = contract(unit, weights[:, 0:width], 1, 0).astype(low).T
        turn[width:] = unit
        keep(0, feats_own[...], grad_own[...], count_a)
        total_turned[...] = jnp.zeros_like(total_turned)
        product[...] = jnp.zeros_like(product)

    def greet(j):
        pl.semaphore_wait(ready.at[j], 1)

        @pl.when(j == beside)
        def _():
            ship(0, across)

        k = z - j // 2 + columns

        @pl.when((lax.rem(j, 2) == x) & (k <= span(j // 2)))
        def _():
            ship(k, {"img": j})

        table_copy(j).start()

    loop(me + 1, n, greet)

    def times(a, k):
        image = me if a == 0 else beside
        peer = peer_of(k)
        listed = table[:, 0, :]
        hits = (listed == image * n + peer) | (listed == peer * n + image)
        return jnp.sum(hits.astype(jnp.float32), keepdims=True)

    def side(scores, slope, live):
        masked = jnp.where(live, scores, NEG_FILL)
        e = jnp.exp(masked - jnp.max(masked, axis=0, keepdims=True))
        inverse = 1.0 / jnp.sum(e, axis=0, keepdims=True)
        weighted = slope * e
        mean = jnp.sum(weighted, axis=0, keepdims=True) * inverse
        d = (weighted - e * mean) * (inverse * scale)
        return (e * inverse).astype(low), d.astype(low)

    def weight_copy(j):
        return push(outgoing.at[j], arrived.at[me], w_send.at[j], w_recv.at[me], {"img": j})

    def term_copy(k):
        device = {"img": peer_of(k)}
        return push(term_out.at[k], term_in.at[k], d_send.at[k], d_recv.at[k], device)

    def last_copy(k, s):
        device = {"img": peer_of(k), "sub": s}
        return push(last_out.at[s], last_in.at[sub], l_send.at[s], l_recv.at[sub], device)

    def swap(k):
        return push(swap_out.at[k], swap_in.at[k], s_send.at[k], s_recv.at[k], partner)

    def each_other(body):
        static_loop(1, n, lambda d: body(lax.rem(me + d, n)))

    def term_of(total):
        return contract(weights[...], total, 1, 0)

    def halve(k, total):
        term = term_of(total)
        for s in range(2):
            term_half[k, s] = term[s * width : (s + 1) * width]
        swap_out[k] = term_half[k, 1 - sub].astype(low)
        swap(k).start()

    def hand_on(k):
        swap(k).wait_recv()
        term_out[k] = (term_half[k, sub] + swap_in[k].astype(jnp.float32)).astype(low)
        term_copy(k).start()

    def slopes_of(k):
        slot = k if held else 0
        peer = peer_of(k)

        @pl.when(k > 0)
        def _():
            ship_feats(k, across).wait_recv()
            core(k, mine).start()
            if held:
                @pl.when(k < end_k - 1)
                def _():
                    table_wait(peer)
            ship_grad(k, across).wait_recv()
            core(k, other).wait_recv()

        count_c = table[peer, 1:2, :]
        count_b = table[beside, 1:2, :]
        block = feats_in[k]
        q, v, g, q_t, g_t, f_t = project(block, grad_in[k], count_c)
        scores = contract(q_rows[...], jnp.concatenate(stack(q), axis=0), 1, 1)
        slopes = contract(v_rows[...], jnp.concatenate(stack(g), axis=0), 1, 1)
        scores_t = contract(q, q_heads[...], 1, 1)
        slopes_t = contract(v, g_heads[...], 1, 1)
        peer_q[slot], peer_g[slot], peer_feats[slot] = q_t, g_t, f_t
        col_live = sublane_ids < count_c
        row_live = [sublane_ids < count_a, sublane_ids < count_b]
        for h in range(heads):
            across_h = slice(h * rows, (h + 1) * rows)
            for a in range(2):
                down = slice(a * rows, (a + 1) * rows)
                cols[slot, down, across_h], dcols[slot, down, across_h] = side(
                    scores[down, across_h], slopes[down, across_h], row_live[a]
                )
                spot = slice((2 * h + a) * rows, (2 * h + a + 1) * rows)
                rows_t[slot, :, spot], drows_t[slot, :, spot] = side(
                    scores_t[:, spot], slopes_t[:, spot], col_live
                )

    def gather_grads(k, final):
        slot = k if held else 0
        factor = jnp.concatenate(
            [jnp.broadcast_to(times(a, k), (1, rows)) for a in range(2)], axis=1
        )
        x_q, x_v, y_q, y_v = [], [], [], []
        for h in range(heads):
            head = slice(h * HEAD_DIM, (h + 1) * HEAD_DIM)
            across_h, spot = slice(h * rows, (h + 1) * rows), slice(2 * h * rows, 2 * (h + 1) * rows)
            col, dcol = cols[slot, :, across_h], dcols[slot, :, across_h]
            row_t, drow_t = rows_t[slot, :, spot], drows_t[slot, :, spot]
            q_a = (q_turned[head].astype(jnp.float32) * factor).astype(low)
            g_a = (g_turned[head].astype(jnp.float32) * factor).astype(low)
            q_c, g_c = peer_q[slot, head], peer_g[slot, head]
            x_q.append(contract(q_c, dcol, 1, 1) + contract(q_c, drow_t, 1, 0))
            x_v.append(contract(g_c, col, 1, 1))
            y_q.append(contract(q_a, dcol, 1, 0) + contract(q_a, drow_t, 1, 1))
            y_v.append(contract(g_a, row_t, 1, 1))
        x_t = jnp.concatenate(x_q + x_v, axis=0) * factor
        y_t = jnp.concatenate(y_q + y_v, axis=0)
        y_low = y_t.astype(low)

        round_it = final & (z + k >= columns)

        @pl.when(round_it)
        def _():
            term = term_of(y_low)
            for s in range(2):
                last_out[s] = term[s * width : (s + 1) * width].astype(low)
                last_copy(k, s).start()

        @pl.when((k > 0) & jnp.logical_not(round_it))
        def _():
            halve(k, y_low)

        weight_term = contract(feats_turned[...], x_t.astype(low), 1, 1)
        weight_term = product[...] + weight_term + contract(peer_feats[slot], y_low, 1, 1)
        if final:
            for c in range(n):
                piece = weight_term[c * share : (c + 1) * share]
                terms[c] = piece
                outgoing[c] = piece.astype(low)
            loop(0, me, lambda j: weight_copy(j).start())
            loop(me + 1, n, lambda j: weight_copy(j).start())
        else:
            product[...] = weight_term
        total_turned[...] += x_t

        @pl.when(k == 0)
        def _():
            total_turned[:, rows:] += y_t

    if n > 1:
        ship_feats(0, across).wait_recv()
        core(0, mine).start()
        table_wait(beside)
        ship_grad(0, across).wait_recv()
        core(0, other).wait_recv()
        keep(1, feats_in[0], grad_in[0], table[beside, 1:2, :])

        def every_table():
            def one(d):
                column = lax.rem(z + d, columns)
                table_wait(column * 2 + 1 - x)
                known = (d < end_k - 1) if held else False

                @pl.when(jnp.logical_not(known))
                def _():
                    table_wait(column * 2 + x)

            loop(1, columns, one)

        if held:
            loop(first_k, end_k - 1, slopes_of)
            every_table()
            loop(first_k, end_k - 1, lambda k: gather_grads(k, False))
        else:
            every_table()

            def step(k):
                slopes_of(k)
                gather_grads(k, False)

                @pl.when(k > 0)
                def _():
                    hand_on(k)

            loop(first_k, end_k - 1, step)
        slopes_of(end_k - 1)
        if held:
            loop(1, jnp.where(z > 0, end_k - 1, 1), hand_on)
        gather_grads(end_k - 1, True)

        @pl.when(z + end_k <= columns)
        def _():
            hand_on(end_k - 1)

        halve(0, total_turned[:, rows:].astype(low))
        halve(columns, total_turned[:, :rows].astype(low))
        hand_on(0)
        if held:
            loop(1, jnp.where(z > 0, 1, end_k - 1), hand_on)
        swap(columns).wait_recv()
        term_own[...] = term_half[columns, sub] + swap_in[columns].astype(jnp.float32)

    def weight_wait(j):
        push(outgoing.at[j], arrived.at[j], w_send.at[j], w_recv.at[j], across).wait_recv()

    each_other(weight_wait)
    total = terms[me]
    for d in range(1, n):
        total = total + arrived[lax.rem(me + d, n)].astype(jnp.float32)
    grad_weights[0] = total[:, :width]
    grad_weights[1] = total[:, width:]

    targets(1, reach + 1, lambda k: sent(k, toward(k)))
    sent(0, across)
    if n > 1:
        each_other(lambda j: table_copy(j).wait_send())
        loop(0, end_k, lambda k: core(k, mine).wait_send())
        each_other(lambda j: weight_copy(j).wait_send())
        swapped = jnp.where(z + end_k > columns, end_k - 1, end_k)
        loop(0, swapped, lambda k: swap(k).wait_send())
        swap(columns).wait_send()
        loop(0, swapped, lambda k: term_copy(k).wait_send())

        @pl.when(z + end_k > columns)
        def _():
            for s in range(2):
                last_copy(end_k - 1, s).wait_send()

    def take(k):
        push(term_out.at[k], term_in.at[k], d_send.at[k], d_recv.at[k], across).wait_recv()
        term_own[...] += term_in[k].astype(jnp.float32)

    def take_either(k):
        sender = lax.rem(z - k + columns, columns)
        ends = (k > z) & (k == span(sender))

        @pl.when(ends)
        def _():
            for s in range(2):
                push(last_out.at[s], last_in.at[s], l_send.at[s], l_recv.at[s], across).wait_recv()
            term_own[...] += last_in[0].astype(jnp.float32) + last_in[1].astype(jnp.float32)

        @pl.when(jnp.logical_not(ends))
        def _():
            take(k)

    take(0)
    targets(1, reach + 1, take_either)
    grad_feats[0] = term_own[...].T.astype(grad_feats.dtype)


def store(feats_from, weights_from, feats_to, weights_to, sem):
    copies = [
        pltpu.make_async_copy(feats_from, feats_to, sem.at[0]),
        pltpu.make_async_copy(weights_from, weights_to, sem.at[1]),
    ]
    for copy in copies:
        copy.start()
    for copy in copies:
        copy.wait()


def local(feats, grad_msg, w_qk, w_v, pair_slots, counts):
    n = lax.axis_size("img")
    columns = n // 2
    held = columns if columns <= HELD_COLUMNS else 1
    rows, depth = feats.shape[1:]
    width = w_qk.shape[1]
    heads = width // HEAD_DIM
    share = depth // n
    slots = pair_slots.shape[1]
    low, full = jnp.bfloat16, jnp.float32
    vmem = pltpu.VMEM
    dma = pltpu.SemaphoreType.DMA
    results = pl.pallas_call(
        functools.partial(kernel, n),
        out_shape=(
            vmem((1, rows, width), low),
            vmem((2, share, width), full),
        ),
        in_specs=[HBM] * 6,
        out_specs=(VMEM,) * 2,
        scratch_shapes=[
            vmem((rows, depth), low),
            vmem((rows, width), low),
            vmem((columns, rows, depth), low),
            vmem((columns, rows, width), low),
            vmem((2, slots), jnp.int32),
            pltpu.SMEM((1,), jnp.int32),
            vmem((n, 2, LANES), jnp.int32),
            vmem((depth, 2 * width), low),
            vmem((width + depth, depth), low),
            vmem((2 * rows, width), low),
            vmem((2 * rows, width), low),
            vmem((2 * heads * rows, width), low),
            vmem((2 * heads * rows, width), low),
            vmem((width, 2 * rows), low),
            vmem((width, 2 * rows), low),
            vmem((depth, 2 * rows), low),
            vmem((2 * width, 2 * rows), full),
            vmem((depth, 2 * width), full),
            vmem((held, 2 * rows, heads * rows), low),
            vmem((held, 2 * rows, heads * rows), low),
            vmem((held, rows, 2 * heads * rows), low),
            vmem((held, rows, 2 * heads * rows), low),
            vmem((held, width, rows), low),
            vmem((held, width, rows), low),
            vmem((held, depth, rows), low),
            vmem((n, share, 2 * width), full),
            vmem((n, share, 2 * width), low),
            vmem((n, share, 2 * width), low),
            vmem((width, rows), full),
            vmem((2, width, rows), low),
            vmem((2, width, rows), low),
            vmem((columns + 1, 2, width, rows), full),
            vmem((columns, width, rows), low),
            vmem((columns, width, rows), low),
            vmem((columns + 1, width, rows), low),
            vmem((columns + 1, width, rows), low),
            dma((6,)), pltpu.SemaphoreType.REGULAR((n,)),
            dma((columns,)), dma((columns,)), dma((columns,)),
            dma((columns,)), dma((columns,)), dma((columns,)),
            dma((n,)), dma((n,)), dma((n,)), dma((n,)),
            dma((columns,)), dma((columns,)), dma((columns + 1,)), dma((columns + 1,)),
            dma((2,)), dma((2,)),
        ],
        compiler_params=pltpu.CompilerParams(
            collective_id=0, has_side_effects=True, vmem_limit_bytes=60 * 1024 * 1024
        ),
        name="backward",
    )(feats, grad_msg, w_qk, w_v, jnp.transpose(pair_slots, (0, 2, 1)), counts)
    any_space = pl.BlockSpec(memory_space=pltpu.VMEM)
    return pl.pallas_call(
        store,
        out_shape=(
            jax.ShapeDtypeStruct((1, rows, width), low),
            jax.ShapeDtypeStruct((2, share, width), full),
        ),
        in_specs=[any_space] * 2,
        out_specs=(pl.BlockSpec(memory_space=pl.ANY),) * 2,
        scratch_shapes=[dma((2,))],
        name="store",
    )(*(pltpu.with_memory_space_constraint(result, pltpu.VMEM) for result in results))


def solution(mesh):
    in_specs = (
        P(("groups", "img"), None, None),
        P(("groups", "img"), None, "sub"),
        P(None, "sub"),
        P(None, "sub"),
        P(("groups", "img"), None, None),
        P(("groups", "img")),
    )
    out_specs = (P(("groups", "img"), None, "sub"), P("groups", "img", "sub"))
    return jax.shard_map(local, mesh=mesh, in_specs=in_specs, out_specs=out_specs, check_vma=False)
```

```python
import functools

import jax
import jax.numpy as jnp
from jax import lax
from jax.experimental import pallas as pl
from jax.experimental.pallas import tpu as pltpu
from jax.sharding import PartitionSpec as P

HEAD_DIM = 64
NEG_FILL = -1e30
LANES = 128
HELD_COLUMNS = 8
MESH = pl.DeviceIdType.MESH
HBM = pl.BlockSpec(memory_space=pltpu.HBM)
VMEM = pl.BlockSpec(memory_space=pltpu.VMEM)


def contract(left, right, left_dim, right_dim):
    return lax.dot_general(
        left, right, (((left_dim,), (right_dim,)), ((), ())), preferred_element_type=jnp.float32
    )


def loop(low, high, body):
    def step(d, carry):
        body(d)
        return carry

    lax.fori_loop(low, high, step, 0)


def static_loop(low, high, body):
    if high - low <= 8:
        for d in range(low, high):
            body(d)
    else:
        loop(low, high, body)


def kernel(
    n, feats, grad, w_qk_in, w_v_in, pairs, counts, grad_feats, grad_weights,
    feats_own, grad_own, feats_in, grad_in, pair_own, count_own, table, weights,
    turn, q_rows, v_rows, q_heads, g_heads, q_turned, g_turned, feats_turned, total_turned, product,
    cols, dcols, rows_t, drows_t, peer_q, peer_g, peer_feats,
    terms, outgoing, arrived, term_own, last_out, last_in, term_half, term_out, term_in, swap_out, swap_in,
    local_sem, ready, f_send, g_send, c_send, f_recv, g_recv, c_recv, t_send, t_recv,
    w_send, w_recv, d_send, d_recv, s_send, s_recv, l_send, l_recv,
):
    me = lax.axis_index("img")
    sub = lax.axis_index("sub")
    columns = n // 2
    held = columns <= HELD_COLUMNS
    z, x = me // 2, lax.rem(me, 2)
    rows = feats.shape[1]
    half = rows // 2
    width = w_qk_in.shape[1]
    heads = width // HEAD_DIM
    scale = HEAD_DIM ** (-0.5)
    share = terms.shape[1]
    depth = feats.shape[2]
    low = jnp.bfloat16
    mine = pl.ds(pl.multiple_of(sub * half, half), half)
    other = pl.ds(pl.multiple_of((1 - sub) * half, half), half)
    beside = me + 1 - 2 * x
    across = {"img": beside}
    partner = {"sub": 1 - sub}
    reach = columns // 2

    def span(column):
        return reach - 1 + jnp.where(column < reach, 1, 0)

    def peer_of(k):
        return jnp.where(k == 0, beside, lax.rem(z + k, columns) * 2 + x)

    def target_of(k):
        return lax.rem(z - k + columns, columns) * 2 + x

    def targets(low_k, high_k, body):
        def one(k):
            @pl.when(k <= span(lax.rem(z - k + columns, columns)))
            def _():
                body(k)

        loop(low_k, high_k, one)

    first_k, end_k = x, span(z) + 1

    barrier = pltpu.get_barrier_semaphore()
    pl.semaphore_signal(barrier, inc=1, device_id=partner, device_id_type=MESH)
    loop(me + 1, n, lambda j: pl.semaphore_signal(
        barrier, inc=1, device_id={"img": j}, device_id_type=MESH
    ))
    own = [
        pltpu.make_async_copy(pairs.at[0], pair_own, local_sem.at[0]),
        pltpu.make_async_copy(counts, count_own, local_sem.at[1]),
        pltpu.make_async_copy(feats.at[0], feats_own, local_sem.at[2]),
        pltpu.make_async_copy(grad.at[0], grad_own, local_sem.at[5]),
        pltpu.make_async_copy(w_qk_in, weights.at[:, pl.ds(0, width)], local_sem.at[3]),
        pltpu.make_async_copy(w_v_in, weights.at[:, pl.ds(width, width)], local_sem.at[4]),
    ]
    for copy in own:
        copy.start()
    pl.semaphore_wait(barrier, me + 1)

    def push(src, dst, send, recv, device):
        return pltpu.make_async_remote_copy(
            src_ref=src, dst_ref=dst, send_sem=send, recv_sem=recv,
            device_id=device, device_id_type=MESH,
        )

    def ship_feats(d, device):
        return push(feats_own.at[mine], feats_in.at[d, mine], f_send.at[d], f_recv.at[d], device)

    def ship_grad(d, device):
        return push(grad_own, grad_in.at[d], g_send.at[d], g_recv.at[d], device)

    def ship(d, device):
        ship_feats(d, device).start()
        ship_grad(d, device).start()

    def sent(d, device):
        ship_feats(d, device).wait_send()
        ship_grad(d, device).wait_send()

    def toward(k):
        return {"img": target_of(k)}

    def core(d, half_rows):
        return push(
            feats_in.at[d, half_rows], feats_in.at[d, half_rows], c_send.at[d], c_recv.at[d], partner
        )

    def table_copy(j):
        return push(table.at[me], table.at[me], t_send.at[j], t_recv.at[me], {"img": j})

    def table_wait(j):
        push(table.at[j], table.at[j], t_send.at[j], t_recv.at[j], {"img": j}).wait_recv()

    loop(0, me, lambda j: pl.semaphore_signal(
        ready.at[me], inc=1, device_id={"img": j}, device_id_type=MESH
    ))
    own[0].wait()
    own[1].wait()
    left, right = pair_own[0:1, :], pair_own[1:2, :]
    count_a = jnp.full((1, LANES), count_own[0], jnp.int32)
    table[me] = jnp.concatenate([jnp.full((1, LANES), -1, jnp.int32), count_a], axis=0)
    table[me, 0:1, 0 : pairs.shape[2]] = jnp.where(left >= 0, left * n + right, -1)
    loop(0, me, lambda j: table_copy(j).start())

    own[2].wait()
    own[3].wait()
    targets(1, jnp.minimum(z, reach) + 1, lambda k: ship(k, toward(k)))

    @pl.when(x == 1)
    def _():
        ship(0, across)


    row_ids = lax.broadcasted_iota(jnp.int32, (rows, width), 0)
    sublane_ids = lax.broadcasted_iota(jnp.int32, (rows, rows), 0)
    unit = lax.broadcasted_iota(jnp.int32, (depth, depth), 0) == lax.broadcasted_iota(jnp.int32, (depth, depth), 1)
    unit = jnp.where(unit, 1.0, 0.0).astype(low)

    def stack(part):
        head = lax.broadcasted_iota(jnp.int32, part.shape, 1) // HEAD_DIM
        zero = jnp.zeros((), part.dtype)
        return [jnp.where(head == h, part, zero) for h in range(heads)]

    def project(block, cotangent, count):
        projected = contract(block, weights[...], 1, 0)
        q = projected[:, :width].astype(low)
        g = jnp.where(row_ids < count, cotangent, jnp.zeros((), low))
        turned = contract(turn[...], block, 1, 1).astype(low)
        g_t = contract(unit[:width, :width], g, 1, 1).astype(low)
        return q, projected[:, width:].astype(low), g, turned[:width], g_t, turned[width:]

    def keep(a, block, cotangent, count):
        q, v, g, q_t, g_t, f_t = project(block, cotangent, count)
        part = slice(a * rows, (a + 1) * rows)
        q = (q.astype(jnp.float32) * scale).astype(low)
        q_rows[part], v_rows[part] = q, v
        for h, (q_part, g_part) in enumerate(zip(stack(q), stack(g))):
            spot = slice((2 * h + a) * rows, (2 * h + a + 1) * rows)
            q_heads[spot], g_heads[spot] = q_part, g_part
        q_turned[:, part], g_turned[:, part], feats_turned[:, part] = q_t, g_t, f_t

    for copy in own[4:]:
        copy.wait()

    if n > 1:
        turn[0:width] = contract(unit, weights[:, 0:width], 1, 0).astype(low).T
        turn[width:] = unit
        keep(0, feats_own[...], grad_own[...], count_a)
        total_turned[...] = jnp.zeros_like(total_turned)
        product[...] = jnp.zeros_like(product)

    def greet(j):
        pl.semaphore_wait(ready.at[j], 1)

        @pl.when(j == beside)
        def _():
            ship(0, across)

        k = z - j // 2 + columns

        @pl.when((lax.rem(j, 2) == x) & (k <= span(j // 2)))
        def _():
            ship(k, {"img": j})

        table_copy(j).start()

    loop(me + 1, n, greet)

    def times(a, k):
        image = me if a == 0 else beside
        peer = peer_of(k)
        listed = table[:, 0, :]
        hits = (listed == image * n + peer) | (listed == peer * n + image)
        return jnp.sum(jnp.sum(hits.astype(jnp.float32), axis=0, keepdims=True), axis=1, keepdims=True)

    def side(scores, slope, live):
        masked = jnp.where(live, scores, NEG_FILL)
        e = jnp.exp(masked - jnp.max(masked, axis=0, keepdims=True))
        inverse = 1.0 / jnp.sum(e, axis=0, keepdims=True)
        weighted = slope * e
        mean = jnp.sum(weighted, axis=0, keepdims=True) * inverse
        d = (weighted - e * mean) * (inverse * scale)
        return (e * inverse).astype(low), d.astype(low)

    def weight_copy(j):
        return push(outgoing.at[j], arrived.at[me], w_send.at[j], w_recv.at[me], {"img": j})

    def term_copy(k):
        device = {"img": peer_of(k)}
        return push(term_out.at[k], term_in.at[k], d_send.at[k], d_recv.at[k], device)

    def last_copy(k, s):
        device = {"img": peer_of(k), "sub": s}
        return push(last_out.at[s], last_in.at[sub], l_send.at[s], l_recv.at[sub], device)

    def swap(k):
        return push(swap_out.at[k], swap_in.at[k], s_send.at[k], s_recv.at[k], partner)

    def each_other(body):
        static_loop(1, n, lambda d: body(lax.rem(me + d, n)))

    def term_of(total):
        return contract(weights[...], total, 1, 0)

    def halve(k, total):
        term = term_of(total)
        for s in range(2):
            term_half[k, s] = term[s * width : (s + 1) * width]
        swap_out[k] = term_half[k, 1 - sub].astype(low)
        swap(k).start()

    def hand_on(k):
        swap(k).wait_recv()
        term_out[k] = (term_half[k, sub] + swap_in[k].astype(jnp.float32)).astype(low)
        term_copy(k).start()

    def slopes_of(k):
        slot = k if held else 0
        peer = peer_of(k)

        @pl.when(k > 0)
        def _():
            ship_feats(k, across).wait_recv()
            core(k, mine).start()
            if held:
                @pl.when(k < end_k - 1)
                def _():
                    table_wait(peer)
            ship_grad(k, across).wait_recv()
            core(k, other).wait_recv()

        count_c = table[peer, 1:2, :]
        count_b = table[beside, 1:2, :]
        block = feats_in[k]
        q, v, g, q_t, g_t, f_t = project(block, grad_in[k], count_c)
        scores = contract(q_rows[...], jnp.concatenate(stack(q), axis=0), 1, 1)
        slopes = contract(v_rows[...], jnp.concatenate(stack(g), axis=0), 1, 1)
        scores_t = contract(q, q_heads[...], 1, 1)
        slopes_t = contract(v, g_heads[...], 1, 1)
        peer_q[slot], peer_g[slot], peer_feats[slot] = q_t, g_t, f_t
        col_live = sublane_ids < count_c
        row_live = [sublane_ids < count_a, sublane_ids < count_b]
        for h in range(heads):
            across_h = slice(h * rows, (h + 1) * rows)
            for a in range(2):
                down = slice(a * rows, (a + 1) * rows)
                cols[slot, down, across_h], dcols[slot, down, across_h] = side(
                    scores[down, across_h], slopes[down, across_h], row_live[a]
                )
                spot = slice((2 * h + a) * rows, (2 * h + a + 1) * rows)
                rows_t[slot, :, spot], drows_t[slot, :, spot] = side(
                    scores_t[:, spot], slopes_t[:, spot], col_live
                )

    def gather_grads(k, final):
        slot = k if held else 0
        factor = jnp.concatenate(
            [jnp.broadcast_to(times(a, k), (1, rows)) for a in range(2)], axis=1
        )
        x_q, x_v, y_q, y_v = [], [], [], []
        for h in range(heads):
            head = slice(h * HEAD_DIM, (h + 1) * HEAD_DIM)
            across_h, spot = slice(h * rows, (h + 1) * rows), slice(2 * h * rows, 2 * (h + 1) * rows)
            col, dcol = cols[slot, :, across_h], dcols[slot, :, across_h]
            row_t, drow_t = rows_t[slot, :, spot], drows_t[slot, :, spot]
            q_a = (q_turned[head].astype(jnp.float32) * factor).astype(low)
            g_a = (g_turned[head].astype(jnp.float32) * factor).astype(low)
            q_c, g_c = peer_q[slot, head], peer_g[slot, head]
            x_q.append(contract(q_c, dcol, 1, 1) + contract(q_c, drow_t, 1, 0))
            x_v.append(contract(g_c, col, 1, 1))
            y_q.append(contract(q_a, dcol, 1, 0) + contract(q_a, drow_t, 1, 1))
            y_v.append(contract(g_a, row_t, 1, 1))
        x_t = jnp.concatenate(x_q + x_v, axis=0) * factor
        y_t = jnp.concatenate(y_q + y_v, axis=0)
        y_low = y_t.astype(low)

        round_it = final & (z + k >= columns)

        @pl.when(round_it)
        def _():
            term = contract(y_low, weights[...], 0, 1)
            for s in range(2):
                last_out[s] = term[:, s * width : (s + 1) * width].astype(low)
                last_copy(k, s).start()

        @pl.when((k > 0) & jnp.logical_not(round_it))
        def _():
            halve(k, y_low)

        weight_term = contract(feats_turned[...], x_t.astype(low), 1, 1)
        weight_term = product[...] + weight_term + contract(peer_feats[slot], y_low, 1, 1)
        if final:
            for c in range(n):
                piece = weight_term[c * share : (c + 1) * share]
                terms[c] = piece
                outgoing[c] = piece.astype(low)
            loop(0, me, lambda j: weight_copy(j).start())
            loop(me + 1, n, lambda j: weight_copy(j).start())
        else:
            product[...] = weight_term
        total_turned[...] += x_t

        @pl.when(k == 0)
        def _():
            total_turned[:, rows:] += y_t

    if n > 1:
        ship_feats(0, across).wait_recv()
        core(0, mine).start()
        table_wait(beside)
        ship_grad(0, across).wait_recv()
        core(0, other).wait_recv()
        keep(1, feats_in[0], grad_in[0], table[beside, 1:2, :])

        def every_table():
            def one(d):
                column = lax.rem(z + d, columns)
                table_wait(column * 2 + 1 - x)
                known = (d < end_k - 1) if held else False

                @pl.when(jnp.logical_not(known))
                def _():
                    table_wait(column * 2 + x)

            loop(1, columns, one)

        if held:
            loop(first_k, end_k - 1, slopes_of)
            every_table()
            loop(first_k, end_k - 1, lambda k: gather_grads(k, False))
        else:
            every_table()

            def step(k):
                slopes_of(k)
                gather_grads(k, False)

                @pl.when(k > 0)
                def _():
                    hand_on(k)

            loop(first_k, end_k - 1, step)
        slopes_of(end_k - 1)
        if held:
            loop(1, jnp.where(z > 0, end_k - 1, 1), hand_on)
        gather_grads(end_k - 1, True)

        @pl.when(z + end_k <= columns)
        def _():
            hand_on(end_k - 1)

        halve(0, total_turned[:, rows:].astype(low))
        halve(columns, total_turned[:, :rows].astype(low))
        hand_on(0)
        if held:
            loop(1, jnp.where(z > 0, 1, end_k - 1), hand_on)
        swap(columns).wait_recv()
        term_own[...] = term_half[columns, sub] + swap_in[columns].astype(jnp.float32)

    def weight_wait(j):
        push(outgoing.at[j], arrived.at[j], w_send.at[j], w_recv.at[j], across).wait_recv()

    each_other(weight_wait)
    total = terms[me]
    for d in range(1, n):
        total = total + arrived[lax.rem(me + d, n)].astype(jnp.float32)
    grad_weights[0] = total[:, :width]
    grad_weights[1] = total[:, width:]

    targets(1, reach + 1, lambda k: sent(k, toward(k)))
    sent(0, across)
    if n > 1:
        each_other(lambda j: table_copy(j).wait_send())
        loop(0, end_k, lambda k: core(k, mine).wait_send())
        each_other(lambda j: weight_copy(j).wait_send())
        swapped = jnp.where(z + end_k > columns, end_k - 1, end_k)
        loop(0, swapped, lambda k: swap(k).wait_send())
        swap(columns).wait_send()
        loop(0, swapped, lambda k: term_copy(k).wait_send())

        @pl.when(z + end_k > columns)
        def _():
            for s in range(2):
                last_copy(end_k - 1, s).wait_send()

    def take(k):
        push(term_out.at[k], term_in.at[k], d_send.at[k], d_recv.at[k], across).wait_recv()
        term_own[...] += term_in[k].astype(jnp.float32)

    def ends(k):
        return (k > z) & (k == span(lax.rem(z - k + columns, columns)))

    def take_summed(k):
        @pl.when(jnp.logical_not(ends(k)))
        def _():
            take(k)

    def take_last(k):
        @pl.when(ends(k))
        def _():
            for s in range(2):
                push(last_out.at[s], last_in.at[s], l_send.at[s], l_recv.at[s], across).wait_recv()
            grad_feats[0] = (
                term_half[columns, 0] + last_in[0].astype(jnp.float32) + last_in[1].astype(jnp.float32)
            ).astype(grad_feats.dtype)

    take(0)
    targets(1, reach + 1, take_summed)
    turned = term_own[...].T
    grad_feats[0] = turned.astype(grad_feats.dtype)
    term_half[columns, 0] = turned
    targets(1, reach + 1, take_last)


def store(feats_from, weights_from, feats_to, weights_to, sem):
    copies = [
        pltpu.make_async_copy(feats_from, feats_to, sem.at[0]),
        pltpu.make_async_copy(weights_from, weights_to, sem.at[1]),
    ]
    for copy in copies:
        copy.start()
    for copy in copies:
        copy.wait()


def local(feats, grad_msg, w_qk, w_v, pair_slots, counts):
    n = lax.axis_size("img")
    columns = n // 2
    held = columns if columns <= HELD_COLUMNS else 1
    rows, depth = feats.shape[1:]
    width = w_qk.shape[1]
    heads = width // HEAD_DIM
    share = depth // n
    slots = pair_slots.shape[1]
    low, full = jnp.bfloat16, jnp.float32
    vmem = pltpu.VMEM
    dma = pltpu.SemaphoreType.DMA
    results = pl.pallas_call(
        functools.partial(kernel, n),
        out_shape=(
            vmem((1, rows, width), low),
            vmem((2, share, width), full),
        ),
        in_specs=[HBM] * 6,
        out_specs=(VMEM,) * 2,
        scratch_shapes=[
            vmem((rows, depth), low),
            vmem((rows, width), low),
            vmem((columns, rows, depth), low),
            vmem((columns, rows, width), low),
            vmem((2, slots), jnp.int32),
            pltpu.SMEM((1,), jnp.int32),
            vmem((n, 2, LANES), jnp.int32),
            vmem((depth, 2 * width), low),
            vmem((width + depth, depth), low),
            vmem((2 * rows, width), low),
            vmem((2 * rows, width), low),
            vmem((2 * heads * rows, width), low),
            vmem((2 * heads * rows, width), low),
            vmem((width, 2 * rows), low),
            vmem((width, 2 * rows), low),
            vmem((depth, 2 * rows), low),
            vmem((2 * width, 2 * rows), full),
            vmem((depth, 2 * width), full),
            vmem((held, 2 * rows, heads * rows), low),
            vmem((held, 2 * rows, heads * rows), low),
            vmem((held, rows, 2 * heads * rows), low),
            vmem((held, rows, 2 * heads * rows), low),
            vmem((held, width, rows), low),
            vmem((held, width, rows), low),
            vmem((held, depth, rows), low),
            vmem((n, share, 2 * width), full),
            vmem((n, share, 2 * width), low),
            vmem((n, share, 2 * width), low),
            vmem((width, rows), full),
            vmem((2, rows, width), low),
            vmem((2, rows, width), low),
            vmem((columns + 1, 2, width, rows), full),
            vmem((columns, width, rows), low),
            vmem((columns, width, rows), low),
            vmem((columns + 1, width, rows), low),
            vmem((columns + 1, width, rows), low),
            dma((6,)), pltpu.SemaphoreType.REGULAR((n,)),
            dma((columns,)), dma((columns,)), dma((columns,)),
            dma((columns,)), dma((columns,)), dma((columns,)),
            dma((n,)), dma((n,)), dma((n,)), dma((n,)),
            dma((columns,)), dma((columns,)), dma((columns + 1,)), dma((columns + 1,)),
            dma((2,)), dma((2,)),
        ],
        compiler_params=pltpu.CompilerParams(
            collective_id=0, has_side_effects=True, vmem_limit_bytes=60 * 1024 * 1024
        ),
        name="backward",
    )(feats, grad_msg, w_qk, w_v, jnp.transpose(pair_slots, (0, 2, 1)), counts)
    any_space = pl.BlockSpec(memory_space=pltpu.VMEM)
    return pl.pallas_call(
        store,
        out_shape=(
            jax.ShapeDtypeStruct((1, rows, width), low),
            jax.ShapeDtypeStruct((2, share, width), full),
        ),
        in_specs=[any_space] * 2,
        out_specs=(pl.BlockSpec(memory_space=pl.ANY),) * 2,
        scratch_shapes=[dma((2,))],
        name="store",
    )(*(pltpu.with_memory_space_constraint(result, pltpu.VMEM) for result in results))


def solution(mesh):
    in_specs = (
        P(("groups", "img"), None, None),
        P(("groups", "img"), None, "sub"),
        P(None, "sub"),
        P(None, "sub"),
        P(("groups", "img"), None, None),
        P(("groups", "img")),
    )
    out_specs = (P(("groups", "img"), None, "sub"), P("groups", "img", "sub"))
    return jax.shard_map(local, mesh=mesh, in_specs=in_specs, out_specs=out_specs, check_vma=False)
```

```python
import functools

import jax
import jax.numpy as jnp
from jax import lax
from jax.experimental import pallas as pl
from jax.experimental.pallas import tpu as pltpu
from jax.sharding import PartitionSpec as P

HEAD_DIM = 64
NEG_FILL = -1e30
LANES = 128
HELD_COLUMNS = 8
MESH = pl.DeviceIdType.MESH
HBM = pl.BlockSpec(memory_space=pltpu.HBM)
VMEM = pl.BlockSpec(memory_space=pltpu.VMEM)


def contract(left, right, left_dim, right_dim):
    return lax.dot_general(
        left, right, (((left_dim,), (right_dim,)), ((), ())), preferred_element_type=jnp.float32
    )


def loop(low, high, body):
    def step(d, carry):
        body(d)
        return carry

    lax.fori_loop(low, high, step, 0)


def static_loop(low, high, body):
    if high - low <= 8:
        for d in range(low, high):
            body(d)
    else:
        loop(low, high, body)


def kernel(
    n, feats, grad, w_qk_in, w_v_in, pairs, counts, grad_feats, grad_weights,
    feats_own, grad_own, feats_in, grad_in, pair_own, count_own, table, weights,
    turn, q_rows, v_rows, q_heads, g_heads, q_turned, g_turned, feats_turned, total_turned, product,
    cols, dcols, rows_t, drows_t, peer_q, peer_g, peer_feats,
    terms, outgoing, arrived, term_own, last_out, last_in, term_half, term_out, term_in, swap_out, swap_in,
    local_sem, ready, f_send, g_send, c_send, f_recv, g_recv, c_recv, t_send, t_recv,
    w_send, w_recv, d_send, d_recv, s_send, s_recv, l_send, l_recv,
):
    me = lax.axis_index("img")
    sub = lax.axis_index("sub")
    columns = n // 2
    held = columns <= HELD_COLUMNS
    z, x = me // 2, lax.rem(me, 2)
    rows = feats.shape[1]
    half = rows // 2
    width = w_qk_in.shape[1]
    heads = width // HEAD_DIM
    scale = HEAD_DIM ** (-0.5)
    share = terms.shape[1]
    depth = feats.shape[2]
    low = jnp.bfloat16
    mine = pl.ds(pl.multiple_of(sub * half, half), half)
    other = pl.ds(pl.multiple_of((1 - sub) * half, half), half)
    beside = me + 1 - 2 * x
    across = {"img": beside}
    partner = {"sub": 1 - sub}
    reach = columns // 2

    def span(column):
        return reach - 1 + jnp.where(column < reach, 1, 0)

    def peer_of(k):
        return jnp.where(k == 0, beside, lax.rem(z + k, columns) * 2 + x)

    def target_of(k):
        return lax.rem(z - k + columns, columns) * 2 + x

    def targets(low_k, high_k, body):
        def one(k):
            @pl.when(k <= span(lax.rem(z - k + columns, columns)))
            def _():
                body(k)

        loop(low_k, high_k, one)

    first_k, end_k = x, span(z) + 1

    barrier = pltpu.get_barrier_semaphore()
    pl.semaphore_signal(barrier, inc=1, device_id=partner, device_id_type=MESH)
    loop(me + 1, n, lambda j: pl.semaphore_signal(
        barrier, inc=1, device_id={"img": j}, device_id_type=MESH
    ))
    own = [
        pltpu.make_async_copy(pairs.at[0], pair_own, local_sem.at[0]),
        pltpu.make_async_copy(counts, count_own, local_sem.at[1]),
        pltpu.make_async_copy(feats.at[0], feats_own, local_sem.at[2]),
        pltpu.make_async_copy(grad.at[0], grad_own, local_sem.at[5]),
        pltpu.make_async_copy(w_qk_in, weights.at[:, pl.ds(0, width)], local_sem.at[3]),
        pltpu.make_async_copy(w_v_in, weights.at[:, pl.ds(width, width)], local_sem.at[4]),
    ]
    for copy in own:
        copy.start()
    pl.semaphore_wait(barrier, me + 1)

    def push(src, dst, send, recv, device):
        return pltpu.make_async_remote_copy(
            src_ref=src, dst_ref=dst, send_sem=send, recv_sem=recv,
            device_id=device, device_id_type=MESH,
        )

    def ship_feats(d, device):
        return push(feats_own.at[mine], feats_in.at[d, mine], f_send.at[d], f_recv.at[d], device)

    def ship_grad(d, device):
        return push(grad_own, grad_in.at[d], g_send.at[d], g_recv.at[d], device)

    def ship(d, device):
        ship_feats(d, device).start()
        ship_grad(d, device).start()

    def sent(d, device):
        ship_feats(d, device).wait_send()
        ship_grad(d, device).wait_send()

    def toward(k):
        return {"img": target_of(k)}

    def core(d, half_rows):
        return push(
            feats_in.at[d, half_rows], feats_in.at[d, half_rows], c_send.at[d], c_recv.at[d], partner
        )

    def table_copy(j):
        return push(table.at[me], table.at[me], t_send.at[j], t_recv.at[me], {"img": j})

    def table_wait(j):
        push(table.at[j], table.at[j], t_send.at[j], t_recv.at[j], {"img": j}).wait_recv()

    loop(0, me, lambda j: pl.semaphore_signal(
        ready.at[me], inc=1, device_id={"img": j}, device_id_type=MESH
    ))
    own[0].wait()
    own[1].wait()
    left, right = pair_own[0:1, :], pair_own[1:2, :]
    count_a = jnp.full((1, LANES), count_own[0], jnp.int32)
    table[me] = jnp.concatenate([jnp.full((1, LANES), -1, jnp.int32), count_a], axis=0)
    table[me, 0:1, 0 : pairs.shape[2]] = jnp.where(left >= 0, left * n + right, -1)
    loop(0, me, lambda j: table_copy(j).start())

    own[2].wait()
    own[3].wait()
    targets(1, jnp.minimum(z, reach) + 1, lambda k: ship(k, toward(k)))

    @pl.when(x == 1)
    def _():
        ship(0, across)


    row_ids = lax.broadcasted_iota(jnp.int32, (rows, width), 0)
    sublane_ids = lax.broadcasted_iota(jnp.int32, (rows, rows), 0)
    unit = lax.broadcasted_iota(jnp.int32, (depth, depth), 0) == lax.broadcasted_iota(jnp.int32, (depth, depth), 1)
    unit = jnp.where(unit, 1.0, 0.0).astype(low)

    def stack(part):
        head = lax.broadcasted_iota(jnp.int32, part.shape, 1) // HEAD_DIM
        zero = jnp.zeros((), part.dtype)
        return [jnp.where(head == h, part, zero) for h in range(heads)]

    def project(block, cotangent, count):
        projected = contract(block, weights[...], 1, 0)
        q = projected[:, :width].astype(low)
        g = jnp.where(row_ids < count, cotangent, jnp.zeros((), low))
        turned = contract(turn[...], block, 1, 1).astype(low)
        g_t = contract(unit[:width, :width], g, 1, 1).astype(low)
        return q, projected[:, width:].astype(low), g, turned[:width], g_t, turned[width:]

    def keep(a, block, cotangent, count):
        q, v, g, q_t, g_t, f_t = project(block, cotangent, count)
        part = slice(a * rows, (a + 1) * rows)
        q = (q.astype(jnp.float32) * scale).astype(low)
        q_rows[part], v_rows[part] = q, v
        for h, (q_part, g_part) in enumerate(zip(stack(q), stack(g))):
            spot = slice((2 * h + a) * rows, (2 * h + a + 1) * rows)
            q_heads[spot], g_heads[spot] = q_part, g_part
        q_turned[:, part], g_turned[:, part], feats_turned[:, part] = q_t, g_t, f_t

    for copy in own[4:]:
        copy.wait()

    if n > 1:
        turn[0:width] = contract(unit, weights[:, 0:width], 1, 0).astype(low).T
        turn[width:] = unit
        keep(0, feats_own[...], grad_own[...], count_a)
        total_turned[...] = jnp.zeros_like(total_turned)
        product[...] = jnp.zeros_like(product)

    def greet(j):
        pl.semaphore_wait(ready.at[j], 1)
        table_copy(j).start()

        @pl.when(j == beside)
        def _():
            ship(0, across)

        k = z - j // 2 + columns

        @pl.when((lax.rem(j, 2) == x) & (k <= span(j // 2)))
        def _():
            ship(k, {"img": j})

    loop(me + 1, n, greet)

    def times(a, k):
        image = me if a == 0 else beside
        peer = peer_of(k)
        listed = table[:, 0, :]
        hits = (listed == image * n + peer) | (listed == peer * n + image)
        return jnp.sum(jnp.sum(hits.astype(jnp.float32), axis=0, keepdims=True), axis=1, keepdims=True)

    def side(scores, slope, live):
        masked = jnp.where(live, scores, NEG_FILL)
        e = jnp.exp(masked - jnp.max(masked, axis=0, keepdims=True))
        inverse = 1.0 / jnp.sum(e, axis=0, keepdims=True)
        weighted = slope * e
        mean = jnp.sum(weighted, axis=0, keepdims=True) * inverse
        d = (weighted - e * mean) * (inverse * scale)
        return (e * inverse).astype(low), d.astype(low)

    def weight_copy(j):
        return push(outgoing.at[j], arrived.at[me], w_send.at[j], w_recv.at[me], {"img": j})

    def term_copy(k):
        device = {"img": peer_of(k)}
        return push(term_out.at[k], term_in.at[k], d_send.at[k], d_recv.at[k], device)

    def last_copy(k, s):
        device = {"img": peer_of(k), "sub": s}
        return push(last_out.at[s], last_in.at[sub], l_send.at[s], l_recv.at[sub], device)

    def swap(k):
        return push(swap_out.at[k], swap_in.at[k], s_send.at[k], s_recv.at[k], partner)

    def each_other(body):
        static_loop(1, n, lambda d: body(lax.rem(me + d, n)))

    def term_of(total):
        return contract(weights[...], total, 1, 0)

    def halve(k, total):
        term = term_of(total)
        for s in range(2):
            term_half[k, s] = term[s * width : (s + 1) * width]
        swap_out[k] = term_half[k, 1 - sub].astype(low)
        swap(k).start()

    def hand_on(k):
        swap(k).wait_recv()
        term_out[k] = (term_half[k, sub] + swap_in[k].astype(jnp.float32)).astype(low)
        term_copy(k).start()

    def slopes_of(k):
        slot = k if held else 0
        peer = peer_of(k)

        @pl.when(k > 0)
        def _():
            ship_feats(k, across).wait_recv()
            core(k, mine).start()
            if held:
                @pl.when(k < end_k - 1)
                def _():
                    table_wait(peer)
            ship_grad(k, across).wait_recv()
            core(k, other).wait_recv()

        count_c = table[peer, 1:2, :]
        count_b = table[beside, 1:2, :]
        block = feats_in[k]
        q, v, g, q_t, g_t, f_t = project(block, grad_in[k], count_c)
        scores = contract(q_rows[...], jnp.concatenate(stack(q), axis=0), 1, 1)
        slopes = contract(v_rows[...], jnp.concatenate(stack(g), axis=0), 1, 1)
        scores_t = contract(q, q_heads[...], 1, 1)
        slopes_t = contract(v, g_heads[...], 1, 1)
        peer_q[slot], peer_g[slot], peer_feats[slot] = q_t, g_t, f_t
        col_live = sublane_ids < count_c
        row_live = [sublane_ids < count_a, sublane_ids < count_b]
        for h in range(heads):
            across_h = slice(h * rows, (h + 1) * rows)
            for a in range(2):
                down = slice(a * rows, (a + 1) * rows)
                cols[slot, down, across_h], dcols[slot, down, across_h] = side(
                    scores[down, across_h], slopes[down, across_h], row_live[a]
                )
                spot = slice((2 * h + a) * rows, (2 * h + a + 1) * rows)
                rows_t[slot, :, spot], drows_t[slot, :, spot] = side(
                    scores_t[:, spot], slopes_t[:, spot], col_live
                )

    def gather_grads(k, final):
        slot = k if held else 0
        factor = jnp.concatenate(
            [jnp.broadcast_to(times(a, k), (1, rows)) for a in range(2)], axis=1
        )
        x_q, x_v, y_q, y_v = [], [], [], []
        for h in range(heads):
            head = slice(h * HEAD_DIM, (h + 1) * HEAD_DIM)
            across_h, spot = slice(h * rows, (h + 1) * rows), slice(2 * h * rows, 2 * (h + 1) * rows)
            col, dcol = cols[slot, :, across_h], dcols[slot, :, across_h]
            row_t, drow_t = rows_t[slot, :, spot], drows_t[slot, :, spot]
            q_a = (q_turned[head].astype(jnp.float32) * factor).astype(low)
            g_a = (g_turned[head].astype(jnp.float32) * factor).astype(low)
            q_c, g_c = peer_q[slot, head], peer_g[slot, head]
            x_q.append(contract(q_c, dcol, 1, 1) + contract(q_c, drow_t, 1, 0))
            x_v.append(contract(g_c, col, 1, 1))
            y_q.append(contract(q_a, dcol, 1, 0) + contract(q_a, drow_t, 1, 1))
            y_v.append(contract(g_a, row_t, 1, 1))
        x_t = jnp.concatenate(x_q + x_v, axis=0) * factor
        y_t = jnp.concatenate(y_q + y_v, axis=0)
        y_low = y_t.astype(low)

        round_it = final & (z + k >= columns)

        @pl.when(round_it)
        def _():
            term = contract(y_low, weights[...], 0, 1)
            for s in range(2):
                last_out[s] = term[:, s * width : (s + 1) * width].astype(low)
                last_copy(k, s).start()

        @pl.when((k > 0) & jnp.logical_not(round_it))
        def _():
            halve(k, y_low)

        weight_term = contract(feats_turned[...], x_t.astype(low), 1, 1)
        weight_term = product[...] + weight_term + contract(peer_feats[slot], y_low, 1, 1)
        if final:
            for c in range(n):
                piece = weight_term[c * share : (c + 1) * share]
                terms[c] = piece
                outgoing[c] = piece.astype(low)
            loop(0, me, lambda j: weight_copy(j).start())
            loop(me + 1, n, lambda j: weight_copy(j).start())
        else:
            product[...] = weight_term
        total_turned[...] += x_t

        @pl.when(k == 0)
        def _():
            total_turned[:, rows:] += y_t

    if n > 1:
        ship_feats(0, across).wait_recv()
        core(0, mine).start()
        table_wait(beside)
        ship_grad(0, across).wait_recv()
        core(0, other).wait_recv()
        keep(1, feats_in[0], grad_in[0], table[beside, 1:2, :])

        def every_table():
            def one(d):
                column = lax.rem(z + d, columns)
                table_wait(column * 2 + 1 - x)
                known = (d < end_k - 1) if held else False

                @pl.when(jnp.logical_not(known))
                def _():
                    table_wait(column * 2 + x)

            loop(1, columns, one)

        if held:
            loop(first_k, end_k - 1, slopes_of)
            every_table()
            loop(first_k, end_k - 1, lambda k: gather_grads(k, False))
        else:
            every_table()

            def step(k):
                slopes_of(k)
                gather_grads(k, False)

                @pl.when(k > 0)
                def _():
                    hand_on(k)

            loop(first_k, end_k - 1, step)
        slopes_of(end_k - 1)
        if held:
            loop(1, jnp.where(z > 0, end_k - 1, 1), hand_on)
        gather_grads(end_k - 1, True)

        @pl.when(z + end_k <= columns)
        def _():
            hand_on(end_k - 1)

        halve(0, total_turned[:, rows:].astype(low))
        halve(columns, total_turned[:, :rows].astype(low))
        hand_on(0)
        if held:
            loop(1, jnp.where(z > 0, 1, end_k - 1), hand_on)
        swap(columns).wait_recv()
        term_own[...] = term_half[columns, sub] + swap_in[columns].astype(jnp.float32)

    def weight_wait(j):
        push(outgoing.at[j], arrived.at[j], w_send.at[j], w_recv.at[j], across).wait_recv()

    each_other(weight_wait)
    total = terms[me]
    for d in range(1, n):
        total = total + arrived[lax.rem(me + d, n)].astype(jnp.float32)
    grad_weights[0] = total[:, :width]
    grad_weights[1] = total[:, width:]

    targets(1, reach + 1, lambda k: sent(k, toward(k)))
    sent(0, across)
    if n > 1:
        each_other(lambda j: table_copy(j).wait_send())
        loop(0, end_k, lambda k: core(k, mine).wait_send())
        each_other(lambda j: weight_copy(j).wait_send())
        swapped = jnp.where(z + end_k > columns, end_k - 1, end_k)
        loop(0, swapped, lambda k: swap(k).wait_send())
        swap(columns).wait_send()
        loop(0, swapped, lambda k: term_copy(k).wait_send())

        @pl.when(z + end_k > columns)
        def _():
            for s in range(2):
                last_copy(end_k - 1, s).wait_send()

    def take(k):
        push(term_out.at[k], term_in.at[k], d_send.at[k], d_recv.at[k], across).wait_recv()
        term_own[...] += term_in[k].astype(jnp.float32)

    def ends(k):
        return (k > z) & (k == span(lax.rem(z - k + columns, columns)))

    def take_summed(k):
        @pl.when(jnp.logical_not(ends(k)))
        def _():
            take(k)

    def take_last(k):
        @pl.when(ends(k))
        def _():
            for s in range(2):
                push(last_out.at[s], last_in.at[s], l_send.at[s], l_recv.at[s], across).wait_recv()
            grad_feats[0] = (
                term_half[columns, 0] + last_in[0].astype(jnp.float32) + last_in[1].astype(jnp.float32)
            ).astype(grad_feats.dtype)

    take(0)
    targets(1, reach + 1, take_summed)
    turned = term_own[...].T
    grad_feats[0] = turned.astype(grad_feats.dtype)
    term_half[columns, 0] = turned
    targets(1, reach + 1, take_last)


def store(feats_from, weights_from, feats_to, weights_to, sem):
    copies = [
        pltpu.make_async_copy(feats_from, feats_to, sem.at[0]),
        pltpu.make_async_copy(weights_from, weights_to, sem.at[1]),
    ]
    for copy in copies:
        copy.start()
    for copy in copies:
        copy.wait()


def local(feats, grad_msg, w_qk, w_v, pair_slots, counts):
    n = lax.axis_size("img")
    columns = n // 2
    held = columns if columns <= HELD_COLUMNS else 1
    rows, depth = feats.shape[1:]
    width = w_qk.shape[1]
    heads = width // HEAD_DIM
    share = depth // n
    slots = pair_slots.shape[1]
    low, full = jnp.bfloat16, jnp.float32
    vmem = pltpu.VMEM
    dma = pltpu.SemaphoreType.DMA
    results = pl.pallas_call(
        functools.partial(kernel, n),
        out_shape=(
            vmem((1, rows, width), low),
            vmem((2, share, width), full),
        ),
        in_specs=[HBM] * 6,
        out_specs=(VMEM,) * 2,
        scratch_shapes=[
            vmem((rows, depth), low),
            vmem((rows, width), low),
            vmem((columns, rows, depth), low),
            vmem((columns, rows, width), low),
            vmem((2, slots), jnp.int32),
            pltpu.SMEM((1,), jnp.int32),
            vmem((n, 2, LANES), jnp.int32),
            vmem((depth, 2 * width), low),
            vmem((width + depth, depth), low),
            vmem((2 * rows, width), low),
            vmem((2 * rows, width), low),
            vmem((2 * heads * rows, width), low),
            vmem((2 * heads * rows, width), low),
            vmem((width, 2 * rows), low),
            vmem((width, 2 * rows), low),
            vmem((depth, 2 * rows), low),
            vmem((2 * width, 2 * rows), full),
            vmem((depth, 2 * width), full),
            vmem((held, 2 * rows, heads * rows), low),
            vmem((held, 2 * rows, heads * rows), low),
            vmem((held, rows, 2 * heads * rows), low),
            vmem((held, rows, 2 * heads * rows), low),
            vmem((held, width, rows), low),
            vmem((held, width, rows), low),
            vmem((held, depth, rows), low),
            vmem((n, share, 2 * width), full),
            vmem((n, share, 2 * width), low),
            vmem((n, share, 2 * width), low),
            vmem((width, rows), full),
            vmem((2, rows, width), low),
            vmem((2, rows, width), low),
            vmem((columns + 1, 2, width, rows), full),
            vmem((columns, width, rows), low),
            vmem((columns, width, rows), low),
            vmem((columns + 1, width, rows), low),
            vmem((columns + 1, width, rows), low),
            dma((6,)), pltpu.SemaphoreType.REGULAR((n,)),
            dma((columns,)), dma((columns,)), dma((columns,)),
            dma((columns,)), dma((columns,)), dma((columns,)),
            dma((n,)), dma((n,)), dma((n,)), dma((n,)),
            dma((columns,)), dma((columns,)), dma((columns + 1,)), dma((columns + 1,)),
            dma((2,)), dma((2,)),
        ],
        compiler_params=pltpu.CompilerParams(
            collective_id=0, has_side_effects=True, vmem_limit_bytes=60 * 1024 * 1024
        ),
        name="backward",
    )(feats, grad_msg, w_qk, w_v, jnp.transpose(pair_slots, (0, 2, 1)), counts)
    any_space = pl.BlockSpec(memory_space=pltpu.VMEM)
    return pl.pallas_call(
        store,
        out_shape=(
            jax.ShapeDtypeStruct((1, rows, width), low),
            jax.ShapeDtypeStruct((2, share, width), full),
        ),
        in_specs=[any_space] * 2,
        out_specs=(pl.BlockSpec(memory_space=pl.ANY),) * 2,
        scratch_shapes=[dma((2,))],
        name="store",
    )(*(pltpu.with_memory_space_constraint(result, pltpu.VMEM) for result in results))


def solution(mesh):
    in_specs = (
        P(("groups", "img"), None, None),
        P(("groups", "img"), None, "sub"),
        P(None, "sub"),
        P(None, "sub"),
        P(("groups", "img"), None, None),
        P(("groups", "img")),
    )
    out_specs = (P(("groups", "img"), None, "sub"), P("groups", "img", "sub"))
    return jax.shard_map(local, mesh=mesh, in_specs=in_specs, out_specs=out_specs, check_vma=False)
```

```python
import functools

import jax
import jax.numpy as jnp
from jax import lax
from jax.experimental import pallas as pl
from jax.experimental.pallas import tpu as pltpu
from jax.sharding import PartitionSpec as P

HEAD_DIM = 64
NEG_FILL = -1e30
LANES = 128
HELD_COLUMNS = 8
MESH = pl.DeviceIdType.MESH
HBM = pl.BlockSpec(memory_space=pltpu.HBM)
VMEM = pl.BlockSpec(memory_space=pltpu.VMEM)


def contract(left, right, left_dim, right_dim):
    return lax.dot_general(
        left, right, (((left_dim,), (right_dim,)), ((), ())), preferred_element_type=jnp.float32
    )


def loop(low, high, body):
    def step(d, carry):
        body(d)
        return carry

    lax.fori_loop(low, high, step, 0)


def static_loop(low, high, body):
    if high - low <= 8:
        for d in range(low, high):
            body(d)
    else:
        loop(low, high, body)


def kernel(
    n, feats, grad, w_qk_in, w_v_in, pairs, counts, grad_feats, grad_weights,
    feats_own, grad_own, feats_in, grad_in, pair_own, table, weights,
    turn, q_rows, v_rows, q_heads, g_heads, q_turned, g_turned, feats_turned, total_turned, product,
    cols, dcols, rows_t, drows_t, peer_q, peer_g, peer_feats,
    terms, outgoing, arrived, term_own, last_out, last_in, term_half, term_out, term_in, swap_out, swap_in,
    local_sem, ready, f_send, g_send, c_send, f_recv, g_recv, c_recv, t_send, t_recv,
    w_send, w_recv, d_send, d_recv, s_send, s_recv, l_send, l_recv,
):
    me = lax.axis_index("img")
    sub = lax.axis_index("sub")
    columns = n // 2
    held = columns <= HELD_COLUMNS
    z, x = me // 2, lax.rem(me, 2)
    rows = feats.shape[1]
    half = rows // 2
    width = w_qk_in.shape[1]
    heads = width // HEAD_DIM
    scale = HEAD_DIM ** (-0.5)
    share = terms.shape[1]
    depth = feats.shape[2]
    low = jnp.bfloat16
    mine = pl.ds(pl.multiple_of(sub * half, half), half)
    other = pl.ds(pl.multiple_of((1 - sub) * half, half), half)
    beside = me + 1 - 2 * x
    across = {"img": beside}
    partner = {"sub": 1 - sub}
    reach = columns // 2

    def span(column):
        return reach - 1 + jnp.where(column < reach, 1, 0)

    def peer_of(k):
        return jnp.where(k == 0, beside, lax.rem(z + k, columns) * 2 + x)

    def target_of(k):
        return lax.rem(z - k + columns, columns) * 2 + x

    def targets(low_k, high_k, body):
        def one(k):
            @pl.when(k <= span(lax.rem(z - k + columns, columns)))
            def _():
                body(k)

        loop(low_k, high_k, one)

    first_k, end_k = x, span(z) + 1

    barrier = pltpu.get_barrier_semaphore()
    pl.semaphore_signal(barrier, inc=1, device_id=partner, device_id_type=MESH)
    loop(me + 1, n, lambda j: pl.semaphore_signal(
        barrier, inc=1, device_id={"img": j}, device_id_type=MESH
    ))
    own = [
        pltpu.make_async_copy(pairs.at[0], pair_own, local_sem.at[0]),
        pltpu.make_async_copy(feats.at[0], feats_own, local_sem.at[2]),
        pltpu.make_async_copy(grad.at[0], grad_own, local_sem.at[5]),
        pltpu.make_async_copy(w_qk_in, weights.at[:, pl.ds(0, width)], local_sem.at[3]),
        pltpu.make_async_copy(w_v_in, weights.at[:, pl.ds(width, width)], local_sem.at[4]),
    ]
    for copy in own:
        copy.start()
    pl.semaphore_wait(barrier, me + 1)

    def push(src, dst, send, recv, device):
        return pltpu.make_async_remote_copy(
            src_ref=src, dst_ref=dst, send_sem=send, recv_sem=recv,
            device_id=device, device_id_type=MESH,
        )

    def ship_feats(d, device):
        return push(feats_own.at[mine], feats_in.at[d, mine], f_send.at[d], f_recv.at[d], device)

    def ship_grad(d, device):
        return push(grad_own, grad_in.at[d], g_send.at[d], g_recv.at[d], device)

    def ship(d, device):
        ship_feats(d, device).start()
        ship_grad(d, device).start()

    def sent(d, device):
        ship_feats(d, device).wait_send()
        ship_grad(d, device).wait_send()

    def toward(k):
        return {"img": target_of(k)}

    def core(d, half_rows):
        return push(
            feats_in.at[d, half_rows], feats_in.at[d, half_rows], c_send.at[d], c_recv.at[d], partner
        )

    def table_copy(j):
        return push(table.at[me], table.at[me], t_send.at[j], t_recv.at[me], {"img": j})

    def table_wait(j):
        push(table.at[j], table.at[j], t_send.at[j], t_recv.at[j], {"img": j}).wait_recv()

    loop(0, me, lambda j: pl.semaphore_signal(
        ready.at[me], inc=1, device_id={"img": j}, device_id_type=MESH
    ))
    own[0].wait()
    left, right = pair_own[0:1, :], pair_own[1:2, :]
    count_a = jnp.full((1, LANES), counts[0], jnp.int32)
    table[me] = jnp.concatenate([jnp.full((1, LANES), -1, jnp.int32), count_a], axis=0)
    table[me, 0:1, 0 : pairs.shape[2]] = jnp.where(left >= 0, left * n + right, -1)
    loop(0, me, lambda j: table_copy(j).start())

    own[1].wait()
    own[2].wait()
    targets(1, jnp.minimum(z, reach) + 1, lambda k: ship(k, toward(k)))

    @pl.when(x == 1)
    def _():
        ship(0, across)


    row_ids = lax.broadcasted_iota(jnp.int32, (rows, width), 0)
    sublane_ids = lax.broadcasted_iota(jnp.int32, (rows, rows), 0)
    unit = lax.broadcasted_iota(jnp.int32, (depth, depth), 0) == lax.broadcasted_iota(jnp.int32, (depth, depth), 1)
    unit = jnp.where(unit, 1.0, 0.0).astype(low)

    def stack(part):
        head = lax.broadcasted_iota(jnp.int32, part.shape, 1) // HEAD_DIM
        zero = jnp.zeros((), part.dtype)
        return [jnp.where(head == h, part, zero) for h in range(heads)]

    def project(block, cotangent, count):
        projected = contract(block, weights[...], 1, 0)
        q = projected[:, :width].astype(low)
        g = jnp.where(row_ids < count, cotangent, jnp.zeros((), low))
        turned = contract(turn[...], block, 1, 1).astype(low)
        g_t = contract(unit[:width, :width], g, 1, 1).astype(low)
        return q, projected[:, width:].astype(low), g, turned[:width], g_t, turned[width:]

    def keep(a, block, cotangent, count):
        q, v, g, q_t, g_t, f_t = project(block, cotangent, count)
        part = slice(a * rows, (a + 1) * rows)
        q = (q.astype(jnp.float32) * scale).astype(low)
        q_rows[part], v_rows[part] = q, v
        for h, (q_part, g_part) in enumerate(zip(stack(q), stack(g))):
            spot = slice((2 * h + a) * rows, (2 * h + a + 1) * rows)
            q_heads[spot], g_heads[spot] = q_part, g_part
        q_turned[:, part], g_turned[:, part], feats_turned[:, part] = q_t, g_t, f_t

    for copy in own[3:]:
        copy.wait()

    if n > 1:
        turn[0:width] = contract(unit, weights[:, 0:width], 1, 0).astype(low).T
        turn[width:] = unit
        keep(0, feats_own[...], grad_own[...], count_a)
        total_turned[...] = jnp.zeros_like(total_turned)
        product[...] = jnp.zeros_like(product)

    def greet(j):
        pl.semaphore_wait(ready.at[j], 1)
        table_copy(j).start()

        @pl.when(j == beside)
        def _():
            ship(0, across)

        k = z - j // 2 + columns

        @pl.when((lax.rem(j, 2) == x) & (k <= span(j // 2)))
        def _():
            ship(k, {"img": j})

    loop(me + 1, n, greet)

    def times(a, k):
        image = me if a == 0 else beside
        peer = peer_of(k)
        listed = table[:, 0, :]
        hits = (listed == image * n + peer) | (listed == peer * n + image)
        return jnp.sum(jnp.sum(hits.astype(jnp.float32), axis=0, keepdims=True), axis=1, keepdims=True)

    def side(scores, slope, live):
        masked = jnp.where(live, scores, NEG_FILL)
        e = jnp.exp(masked - jnp.max(masked, axis=0, keepdims=True))
        inverse = 1.0 / jnp.sum(e, axis=0, keepdims=True)
        weighted = slope * e
        mean = jnp.sum(weighted, axis=0, keepdims=True) * inverse
        d = (weighted - e * mean) * (inverse * scale)
        return (e * inverse).astype(low), d.astype(low)

    def weight_copy(j):
        return push(outgoing.at[j], arrived.at[me], w_send.at[j], w_recv.at[me], {"img": j})

    def term_copy(k):
        device = {"img": peer_of(k)}
        return push(term_out.at[k], term_in.at[k], d_send.at[k], d_recv.at[k], device)

    def last_copy(k, s):
        device = {"img": peer_of(k), "sub": s}
        return push(last_out.at[s], last_in.at[sub], l_send.at[s], l_recv.at[sub], device)

    def swap(k):
        return push(swap_out.at[k], swap_in.at[k], s_send.at[k], s_recv.at[k], partner)

    def each_other(body):
        static_loop(1, n, lambda d: body(lax.rem(me + d, n)))

    def term_of(total):
        return contract(weights[...], total, 1, 0)

    def halve(k, total):
        term = term_of(total)
        for s in range(2):
            term_half[k, s] = term[s * width : (s + 1) * width]
        swap_out[k] = term_half[k, 1 - sub].astype(low)
        swap(k).start()

    def hand_on(k):
        swap(k).wait_recv()
        term_out[k] = (term_half[k, sub] + swap_in[k].astype(jnp.float32)).astype(low)
        term_copy(k).start()

    def slopes_of(k):
        slot = k if held else 0
        peer = peer_of(k)

        @pl.when(k > 0)
        def _():
            ship_feats(k, across).wait_recv()
            core(k, mine).start()
            if held:
                @pl.when(k < end_k - 1)
                def _():
                    table_wait(peer)
            ship_grad(k, across).wait_recv()
            core(k, other).wait_recv()

        count_c = table[peer, 1:2, :]
        count_b = table[beside, 1:2, :]
        block = feats_in[k]
        q, v, g, q_t, g_t, f_t = project(block, grad_in[k], count_c)
        scores = contract(q_rows[...], jnp.concatenate(stack(q), axis=0), 1, 1)
        slopes = contract(v_rows[...], jnp.concatenate(stack(g), axis=0), 1, 1)
        scores_t = contract(q, q_heads[...], 1, 1)
        slopes_t = contract(v, g_heads[...], 1, 1)
        peer_q[slot], peer_g[slot], peer_feats[slot] = q_t, g_t, f_t
        col_live = sublane_ids < count_c
        row_live = [sublane_ids < count_a, sublane_ids < count_b]
        for h in range(heads):
            across_h = slice(h * rows, (h + 1) * rows)
            for a in range(2):
                down = slice(a * rows, (a + 1) * rows)
                cols[slot, down, across_h], dcols[slot, down, across_h] = side(
                    scores[down, across_h], slopes[down, across_h], row_live[a]
                )
                spot = slice((2 * h + a) * rows, (2 * h + a + 1) * rows)
                rows_t[slot, :, spot], drows_t[slot, :, spot] = side(
                    scores_t[:, spot], slopes_t[:, spot], col_live
                )

    def gather_grads(k, final):
        slot = k if held else 0
        factor = jnp.concatenate(
            [jnp.broadcast_to(times(a, k), (1, rows)) for a in range(2)], axis=1
        )
        x_q, x_v, y_q, y_v = [], [], [], []
        for h in range(heads):
            head = slice(h * HEAD_DIM, (h + 1) * HEAD_DIM)
            across_h, spot = slice(h * rows, (h + 1) * rows), slice(2 * h * rows, 2 * (h + 1) * rows)
            col, dcol = cols[slot, :, across_h], dcols[slot, :, across_h]
            row_t, drow_t = rows_t[slot, :, spot], drows_t[slot, :, spot]
            q_a = (q_turned[head].astype(jnp.float32) * factor).astype(low)
            g_a = (g_turned[head].astype(jnp.float32) * factor).astype(low)
            q_c, g_c = peer_q[slot, head], peer_g[slot, head]
            x_q.append(contract(q_c, dcol, 1, 1) + contract(q_c, drow_t, 1, 0))
            x_v.append(contract(g_c, col, 1, 1))
            y_q.append(contract(q_a, dcol, 1, 0) + contract(q_a, drow_t, 1, 1))
            y_v.append(contract(g_a, row_t, 1, 1))
        x_t = jnp.concatenate(x_q + x_v, axis=0) * factor
        y_t = jnp.concatenate(y_q + y_v, axis=0)
        y_low = y_t.astype(low)

        round_it = final & (z + k >= columns)

        @pl.when(round_it)
        def _():
            term = contract(y_low, weights[...], 0, 1)
            for s in range(2):
                last_out[s] = term[:, s * width : (s + 1) * width].astype(low)
                last_copy(k, s).start()

        @pl.when((k > 0) & jnp.logical_not(round_it))
        def _():
            halve(k, y_low)

        weight_term = contract(feats_turned[...], x_t.astype(low), 1, 1)
        weight_term = product[...] + weight_term + contract(peer_feats[slot], y_low, 1, 1)
        if final:
            for c in range(n):
                piece = weight_term[c * share : (c + 1) * share]
                terms[c] = piece
                outgoing[c] = piece.astype(low)
            loop(0, me, lambda j: weight_copy(j).start())
            loop(me + 1, n, lambda j: weight_copy(j).start())
        else:
            product[...] = weight_term
        total_turned[...] += x_t

        @pl.when(k == 0)
        def _():
            total_turned[:, rows:] += y_t

    if n > 1:
        ship_feats(0, across).wait_recv()
        core(0, mine).start()
        table_wait(beside)
        ship_grad(0, across).wait_recv()
        core(0, other).wait_recv()
        keep(1, feats_in[0], grad_in[0], table[beside, 1:2, :])

        def every_table():
            def one(d):
                column = lax.rem(z + d, columns)
                table_wait(column * 2 + 1 - x)
                known = (d < end_k - 1) if held else False

                @pl.when(jnp.logical_not(known))
                def _():
                    table_wait(column * 2 + x)

            loop(1, columns, one)

        if held:
            loop(first_k, end_k - 1, slopes_of)
            every_table()
            loop(first_k, end_k - 1, lambda k: gather_grads(k, False))
        else:
            every_table()

            def step(k):
                slopes_of(k)
                gather_grads(k, False)

                @pl.when(k > 0)
                def _():
                    hand_on(k)

            loop(first_k, end_k - 1, step)
        slopes_of(end_k - 1)
        if held:
            loop(1, jnp.where(z > 0, end_k - 1, 1), hand_on)
        gather_grads(end_k - 1, True)

        @pl.when(z + end_k <= columns)
        def _():
            hand_on(end_k - 1)

        halve(0, total_turned[:, rows:].astype(low))
        halve(columns, total_turned[:, :rows].astype(low))
        hand_on(0)
        if held:
            loop(1, jnp.where(z > 0, 1, end_k - 1), hand_on)
        swap(columns).wait_recv()
        term_own[...] = term_half[columns, sub] + swap_in[columns].astype(jnp.float32)

    def weight_wait(j):
        push(outgoing.at[j], arrived.at[j], w_send.at[j], w_recv.at[j], across).wait_recv()

    each_other(weight_wait)
    total = terms[me]
    for d in range(1, n):
        total = total + arrived[lax.rem(me + d, n)].astype(jnp.float32)
    grad_weights[0] = total[:, :width]
    grad_weights[1] = total[:, width:]

    targets(1, reach + 1, lambda k: sent(k, toward(k)))
    sent(0, across)
    if n > 1:
        each_other(lambda j: table_copy(j).wait_send())
        loop(0, end_k, lambda k: core(k, mine).wait_send())
        each_other(lambda j: weight_copy(j).wait_send())
        swapped = jnp.where(z + end_k > columns, end_k - 1, end_k)
        loop(0, swapped, lambda k: swap(k).wait_send())
        swap(columns).wait_send()
        loop(0, swapped, lambda k: term_copy(k).wait_send())

        @pl.when(z + end_k > columns)
        def _():
            for s in range(2):
                last_copy(end_k - 1, s).wait_send()

    def take(k):
        push(term_out.at[k], term_in.at[k], d_send.at[k], d_recv.at[k], across).wait_recv()
        term_own[...] += term_in[k].astype(jnp.float32)

    def ends(k):
        return (k > z) & (k == span(lax.rem(z - k + columns, columns)))

    def take_summed(k):
        @pl.when(jnp.logical_not(ends(k)))
        def _():
            take(k)

    def take_last(k):
        @pl.when(ends(k))
        def _():
            for s in range(2):
                push(last_out.at[s], last_in.at[s], l_send.at[s], l_recv.at[s], across).wait_recv()
            grad_feats[0] = (
                term_half[columns, 0] + last_in[0].astype(jnp.float32) + last_in[1].astype(jnp.float32)
            ).astype(grad_feats.dtype)

    take(0)
    targets(1, reach + 1, take_summed)
    turned = term_own[...].T
    grad_feats[0] = turned.astype(grad_feats.dtype)
    term_half[columns, 0] = turned
    targets(1, reach + 1, take_last)


def store(feats_from, weights_from, feats_to, weights_to, sem):
    copies = [
        pltpu.make_async_copy(feats_from, feats_to, sem.at[0]),
        pltpu.make_async_copy(weights_from, weights_to, sem.at[1]),
    ]
    for copy in copies:
        copy.start()
    for copy in copies:
        copy.wait()


def local(feats, grad_msg, w_qk, w_v, pair_slots, counts):
    n = lax.axis_size("img")
    columns = n // 2
    held = columns if columns <= HELD_COLUMNS else 1
    rows, depth = feats.shape[1:]
    width = w_qk.shape[1]
    heads = width // HEAD_DIM
    share = depth // n
    slots = pair_slots.shape[1]
    low, full = jnp.bfloat16, jnp.float32
    vmem = pltpu.VMEM
    dma = pltpu.SemaphoreType.DMA
    results = pl.pallas_call(
        functools.partial(kernel, n),
        out_shape=(
            vmem((1, rows, width), low),
            vmem((2, share, width), full),
        ),
        in_specs=[HBM] * 5 + [pl.BlockSpec(memory_space=pltpu.SMEM)],
        out_specs=(VMEM,) * 2,
        scratch_shapes=[
            vmem((rows, depth), low),
            vmem((rows, width), low),
            vmem((columns, rows, depth), low),
            vmem((columns, rows, width), low),
            vmem((2, slots), jnp.int32),
            vmem((n, 2, LANES), jnp.int32),
            vmem((depth, 2 * width), low),
            vmem((width + depth, depth), low),
            vmem((2 * rows, width), low),
            vmem((2 * rows, width), low),
            vmem((2 * heads * rows, width), low),
            vmem((2 * heads * rows, width), low),
            vmem((width, 2 * rows), low),
            vmem((width, 2 * rows), low),
            vmem((depth, 2 * rows), low),
            vmem((2 * width, 2 * rows), full),
            vmem((depth, 2 * width), full),
            vmem((held, 2 * rows, heads * rows), low),
            vmem((held, 2 * rows, heads * rows), low),
            vmem((held, rows, 2 * heads * rows), low),
            vmem((held, rows, 2 * heads * rows), low),
            vmem((held, width, rows), low),
            vmem((held, width, rows), low),
            vmem((held, depth, rows), low),
            vmem((n, share, 2 * width), full),
            vmem((n, share, 2 * width), low),
            vmem((n, share, 2 * width), low),
            vmem((width, rows), full),
            vmem((2, rows, width), low),
            vmem((2, rows, width), low),
            vmem((columns + 1, 2, width, rows), full),
            vmem((columns, width, rows), low),
            vmem((columns, width, rows), low),
            vmem((columns + 1, width, rows), low),
            vmem((columns + 1, width, rows), low),
            dma((6,)), pltpu.SemaphoreType.REGULAR((n,)),
            dma((columns,)), dma((columns,)), dma((columns,)),
            dma((columns,)), dma((columns,)), dma((columns,)),
            dma((n,)), dma((n,)), dma((n,)), dma((n,)),
            dma((columns,)), dma((columns,)), dma((columns + 1,)), dma((columns + 1,)),
            dma((2,)), dma((2,)),
        ],
        compiler_params=pltpu.CompilerParams(
            collective_id=0, has_side_effects=True, vmem_limit_bytes=60 * 1024 * 1024
        ),
        name="backward",
    )(feats, grad_msg, w_qk, w_v, jnp.transpose(pair_slots, (0, 2, 1)), counts)
    any_space = pl.BlockSpec(memory_space=pltpu.VMEM)
    return pl.pallas_call(
        store,
        out_shape=(
            jax.ShapeDtypeStruct((1, rows, width), low),
            jax.ShapeDtypeStruct((2, share, width), full),
        ),
        in_specs=[any_space] * 2,
        out_specs=(pl.BlockSpec(memory_space=pl.ANY),) * 2,
        scratch_shapes=[dma((2,))],
        name="store",
    )(*(pltpu.with_memory_space_constraint(result, pltpu.VMEM) for result in results))


def solution(mesh):
    in_specs = (
        P(("groups", "img"), None, None),
        P(("groups", "img"), None, "sub"),
        P(None, "sub"),
        P(None, "sub"),
        P(("groups", "img"), None, None),
        P(("groups", "img")),
    )
    out_specs = (P(("groups", "img"), None, "sub"), P("groups", "img", "sub"))
    return jax.shard_map(local, mesh=mesh, in_specs=in_specs, out_specs=out_specs, check_vma=False)
```

```python
import functools

import jax
import jax.numpy as jnp
from jax import lax
from jax.experimental import pallas as pl
from jax.experimental.pallas import tpu as pltpu
from jax.sharding import PartitionSpec as P

HEAD_DIM = 64
NEG_FILL = -1e30
LANES = 128
HELD_COLUMNS = 8
MESH = pl.DeviceIdType.MESH
HBM = pl.BlockSpec(memory_space=pltpu.HBM)
VMEM = pl.BlockSpec(memory_space=pltpu.VMEM)


def contract(left, right, left_dim, right_dim):
    return lax.dot_general(
        left, right, (((left_dim,), (right_dim,)), ((), ())), preferred_element_type=jnp.float32
    )


def loop(low, high, body):
    def step(d, carry):
        body(d)
        return carry

    lax.fori_loop(low, high, step, 0)


def static_loop(low, high, body):
    if high - low <= 8:
        for d in range(low, high):
            body(d)
    else:
        loop(low, high, body)


def kernel(
    n, feats, grad, w_qk_in, w_v_in, pairs, counts, grad_feats, grad_weights,
    feats_own, grad_own, feats_in, grad_in, pair_own, count_own, table, weights,
    turn, q_rows, v_rows, q_heads, g_heads, q_turned, g_turned, feats_turned, total_turned, product,
    cols, dcols, rows_t, drows_t, peer_q, peer_g, peer_feats,
    terms, outgoing, arrived, term_own, last_out, last_in, term_half, term_out, term_in, swap_out, swap_in,
    local_sem, ready, f_send, g_send, c_send, f_recv, g_recv, c_recv, t_send, t_recv,
    w_send, w_recv, d_send, d_recv, s_send, s_recv, l_send, l_recv,
):
    me = lax.axis_index("img")
    sub = lax.axis_index("sub")
    columns = n // 2
    held = columns <= HELD_COLUMNS
    z, x = me // 2, lax.rem(me, 2)
    rows = feats.shape[1]
    half = rows // 2
    width = w_qk_in.shape[1]
    heads = width // HEAD_DIM
    scale = HEAD_DIM ** (-0.5)
    share = terms.shape[1]
    depth = feats.shape[2]
    low = jnp.bfloat16
    mine = pl.ds(pl.multiple_of(sub * half, half), half)
    other = pl.ds(pl.multiple_of((1 - sub) * half, half), half)
    beside = me + 1 - 2 * x
    across = {"img": beside}
    partner = {"sub": 1 - sub}
    reach = columns // 2

    def span(column):
        return reach - 1 + jnp.where(column < reach, 1, 0)

    def peer_of(k):
        return jnp.where(k == 0, beside, lax.rem(z + k, columns) * 2 + x)

    def target_of(k):
        return lax.rem(z - k + columns, columns) * 2 + x

    def targets(low_k, high_k, body):
        def one(k):
            @pl.when(k <= span(lax.rem(z - k + columns, columns)))
            def _():
                body(k)

        loop(low_k, high_k, one)

    first_k, end_k = x, span(z) + 1

    barrier = pltpu.get_barrier_semaphore()
    pl.semaphore_signal(barrier, inc=1, device_id=partner, device_id_type=MESH)
    loop(me + 1, n, lambda j: pl.semaphore_signal(
        barrier, inc=1, device_id={"img": j}, device_id_type=MESH
    ))
    own = [
        pltpu.make_async_copy(pairs.at[0], pair_own, local_sem.at[0]),
        pltpu.make_async_copy(counts, count_own, local_sem.at[1]),
        pltpu.make_async_copy(feats.at[0], feats_own, local_sem.at[2]),
        pltpu.make_async_copy(grad.at[0], grad_own, local_sem.at[5]),
        pltpu.make_async_copy(w_qk_in, weights.at[:, pl.ds(0, width)], local_sem.at[3]),
        pltpu.make_async_copy(w_v_in, weights.at[:, pl.ds(width, width)], local_sem.at[4]),
    ]
    for copy in own:
        copy.start()
    pl.semaphore_wait(barrier, me + 1)

    def push(src, dst, send, recv, device):
        return pltpu.make_async_remote_copy(
            src_ref=src, dst_ref=dst, send_sem=send, recv_sem=recv,
            device_id=device, device_id_type=MESH,
        )

    def ship_feats(d, device):
        return push(feats_own.at[mine], feats_in.at[d, mine], f_send.at[d], f_recv.at[d], device)

    def ship_grad(d, device):
        return push(grad_own, grad_in.at[d], g_send.at[d], g_recv.at[d], device)

    def ship(d, device):
        ship_feats(d, device).start()
        ship_grad(d, device).start()

    def sent(d, device):
        ship_feats(d, device).wait_send()
        ship_grad(d, device).wait_send()

    def toward(k):
        return {"img": target_of(k)}

    def core(d, half_rows):
        return push(
            feats_in.at[d, half_rows], feats_in.at[d, half_rows], c_send.at[d], c_recv.at[d], partner
        )

    def table_copy(j):
        return push(table.at[me], table.at[me], t_send.at[j], t_recv.at[me], {"img": j})

    def table_wait(j):
        push(table.at[j], table.at[j], t_send.at[j], t_recv.at[j], {"img": j}).wait_recv()

    loop(0, me, lambda j: pl.semaphore_signal(
        ready.at[me], inc=1, device_id={"img": j}, device_id_type=MESH
    ))
    own[0].wait()
    own[1].wait()
    left, right = pair_own[0:1, :], pair_own[1:2, :]
    count_a = jnp.full((1, LANES), count_own[0], jnp.int32)
    table[me] = jnp.concatenate([jnp.full((1, LANES), -1, jnp.int32), count_a], axis=0)
    table[me, 0:1, 0 : pairs.shape[2]] = jnp.where(left >= 0, left * n + right, -1)
    loop(0, me, lambda j: table_copy(j).start())

    own[2].wait()
    own[3].wait()
    targets(1, jnp.minimum(z, reach) + 1, lambda k: ship(k, toward(k)))

    @pl.when(x == 1)
    def _():
        ship(0, across)


    row_ids = lax.broadcasted_iota(jnp.int32, (rows, width), 0)
    sublane_ids = lax.broadcasted_iota(jnp.int32, (rows, rows), 0)
    unit = lax.broadcasted_iota(jnp.int32, (depth, depth), 0) == lax.broadcasted_iota(jnp.int32, (depth, depth), 1)
    unit = jnp.where(unit, 1.0, 0.0).astype(low)

    def stack(part):
        head = lax.broadcasted_iota(jnp.int32, part.shape, 1) // HEAD_DIM
        zero = jnp.zeros((), part.dtype)
        return [jnp.where(head == h, part, zero) for h in range(heads)]

    def project(block, cotangent, count):
        projected = contract(block, weights[...], 1, 0)
        q = projected[:, :width].astype(low)
        g = jnp.where(row_ids < count, cotangent, jnp.zeros((), low))
        turned = contract(turn[...], block, 1, 1).astype(low)
        g_t = contract(unit[:width, :width], g, 1, 1).astype(low)
        return q, projected[:, width:].astype(low), g, turned[:width], g_t, turned[width:]

    def keep(a, block, cotangent, count):
        q, v, g, q_t, g_t, f_t = project(block, cotangent, count)
        part = slice(a * rows, (a + 1) * rows)
        q = (q.astype(jnp.float32) * scale).astype(low)
        q_rows[part], v_rows[part] = q, v
        for h, (q_part, g_part) in enumerate(zip(stack(q), stack(g))):
            spot = slice((2 * h + a) * rows, (2 * h + a + 1) * rows)
            q_heads[spot], g_heads[spot] = q_part, g_part
        q_turned[:, part], g_turned[:, part], feats_turned[:, part] = q_t, g_t, f_t

    for copy in own[4:]:
        copy.wait()

    if n > 1:
        turn[0:width] = contract(unit, weights[:, 0:width], 1, 0).astype(low).T
        turn[width:] = unit
        keep(0, feats_own[...], grad_own[...], count_a)
        total_turned[...] = jnp.zeros_like(total_turned)
        product[...] = jnp.zeros_like(product)

    def greet(j):
        pl.semaphore_wait(ready.at[j], 1)
        table_copy(j).start()

        @pl.when(j == beside)
        def _():
            ship(0, across)

        k = z - j // 2 + columns

        @pl.when((lax.rem(j, 2) == x) & (k <= span(j // 2)))
        def _():
            ship(k, {"img": j})

    loop(me + 1, n, greet)

    def times(a, k):
        image = me if a == 0 else beside
        peer = peer_of(k)
        listed = table[:, 0, :]
        hits = (listed == image * n + peer) | (listed == peer * n + image)
        return jnp.sum(jnp.sum(hits.astype(jnp.float32), axis=0, keepdims=True), axis=1, keepdims=True)

    def side(scores, slope, live):
        masked = jnp.where(live, scores, NEG_FILL)
        e = jnp.exp(masked - jnp.max(masked, axis=0, keepdims=True))
        inverse = 1.0 / jnp.sum(e, axis=0, keepdims=True)
        weighted = slope * e
        mean = jnp.sum(weighted, axis=0, keepdims=True) * inverse
        d = (weighted - e * mean) * (inverse * scale)
        return (e * inverse).astype(low), d.astype(low)

    def weight_copy(j):
        return push(outgoing.at[j], arrived.at[me], w_send.at[j], w_recv.at[me], {"img": j})

    def term_copy(k):
        device = {"img": peer_of(k)}
        return push(term_out.at[k], term_in.at[k], d_send.at[k], d_recv.at[k], device)

    def last_copy(k, s):
        device = {"img": peer_of(k), "sub": s}
        return push(last_out.at[s], last_in.at[sub], l_send.at[s], l_recv.at[sub], device)

    def swap(k):
        return push(swap_out.at[k], swap_in.at[k], s_send.at[k], s_recv.at[k], partner)

    def each_other(body):
        static_loop(1, n, lambda d: body(lax.rem(me + d, n)))

    def term_of(total):
        return contract(weights[...], total, 1, 0)

    def halve(k, total):
        term = term_of(total)
        for s in range(2):
            term_half[k, s] = term[s * width : (s + 1) * width]
        swap_out[k] = term_half[k, 1 - sub].astype(low)
        swap(k).start()

    def hand_on(k):
        swap(k).wait_recv()
        term_out[k] = (term_half[k, sub] + swap_in[k].astype(jnp.float32)).astype(low)
        term_copy(k).start()

    def slopes_of(k):
        slot = k if held else 0
        peer = peer_of(k)

        @pl.when(k > 0)
        def _():
            ship_feats(k, across).wait_recv()
            core(k, mine).start()
            if held:
                @pl.when(k < end_k - 1)
                def _():
                    table_wait(peer)
            ship_grad(k, across).wait_recv()
            core(k, other).wait_recv()

        count_c = table[peer, 1:2, :]
        count_b = table[beside, 1:2, :]
        block = feats_in[k]
        q, v, g, q_t, g_t, f_t = project(block, grad_in[k], count_c)
        scores = contract(q_rows[...], jnp.concatenate(stack(q), axis=0), 1, 1)
        slopes = contract(v_rows[...], jnp.concatenate(stack(g), axis=0), 1, 1)
        scores_t = contract(q, q_heads[...], 1, 1)
        slopes_t = contract(v, g_heads[...], 1, 1)
        peer_q[slot], peer_g[slot], peer_feats[slot] = q_t, g_t, f_t
        col_live = sublane_ids < count_c
        row_live = [sublane_ids < count_a, sublane_ids < count_b]
        for h in range(heads):
            across_h = slice(h * rows, (h + 1) * rows)
            for a in range(2):
                down = slice(a * rows, (a + 1) * rows)
                cols[slot, down, across_h], dcols[slot, down, across_h] = side(
                    scores[down, across_h], slopes[down, across_h], row_live[a]
                )
                spot = slice((2 * h + a) * rows, (2 * h + a + 1) * rows)
                rows_t[slot, :, spot], drows_t[slot, :, spot] = side(
                    scores_t[:, spot], slopes_t[:, spot], col_live
                )

    def gather_grads(k, final):
        slot = k if held else 0
        factor = jnp.concatenate(
            [jnp.broadcast_to(times(a, k), (1, rows)) for a in range(2)], axis=1
        )
        x_q, x_v, y_q, y_v = [], [], [], []
        for h in range(heads):
            head = slice(h * HEAD_DIM, (h + 1) * HEAD_DIM)
            across_h, spot = slice(h * rows, (h + 1) * rows), slice(2 * h * rows, 2 * (h + 1) * rows)
            col, dcol = cols[slot, :, across_h], dcols[slot, :, across_h]
            row_t, drow_t = rows_t[slot, :, spot], drows_t[slot, :, spot]
            q_a = (q_turned[head].astype(jnp.float32) * factor).astype(low)
            g_a = (g_turned[head].astype(jnp.float32) * factor).astype(low)
            q_c, g_c = peer_q[slot, head], peer_g[slot, head]
            x_q.append(contract(q_c, dcol, 1, 1) + contract(q_c, drow_t, 1, 0))
            x_v.append(contract(g_c, col, 1, 1))
            y_q.append(contract(q_a, dcol, 1, 0) + contract(q_a, drow_t, 1, 1))
            y_v.append(contract(g_a, row_t, 1, 1))
        x_t = jnp.concatenate(x_q + x_v, axis=0) * factor
        y_t = jnp.concatenate(y_q + y_v, axis=0)
        y_low = y_t.astype(low)

        round_it = final & (z + k >= columns)

        @pl.when(round_it)
        def _():
            term = contract(y_low, weights[...], 0, 1)
            for s in range(2):
                last_out[s] = term[:, s * width : (s + 1) * width].astype(low)
                last_copy(k, s).start()

        @pl.when((k > 0) & jnp.logical_not(round_it))
        def _():
            halve(k, y_low)

        weight_term = contract(feats_turned[...], x_t.astype(low), 1, 1)
        weight_term = product[...] + weight_term + contract(peer_feats[slot], y_low, 1, 1)
        if final:
            for c in range(n):
                piece = weight_term[c * share : (c + 1) * share]
                terms[c] = piece
                outgoing[c] = piece.astype(low)
            loop(0, me, lambda j: weight_copy(j).start())
            loop(me + 1, n, lambda j: weight_copy(j).start())
        else:
            product[...] = weight_term
        total_turned[...] += x_t

        @pl.when(k == 0)
        def _():
            total_turned[:, rows:] += y_t

    if n > 1:
        ship_feats(0, across).wait_recv()
        core(0, mine).start()
        table_wait(beside)
        ship_grad(0, across).wait_recv()
        core(0, other).wait_recv()
        keep(1, feats_in[0], grad_in[0], table[beside, 1:2, :])

        def every_table():
            def one(d):
                column = lax.rem(z + d, columns)
                table_wait(column * 2 + 1 - x)
                known = (d < end_k - 1) if held else False

                @pl.when(jnp.logical_not(known))
                def _():
                    table_wait(column * 2 + x)

            loop(1, columns, one)

        if held:
            loop(first_k, end_k - 1, slopes_of)
            every_table()
            loop(first_k, end_k - 1, lambda k: gather_grads(k, False))
        else:
            every_table()

            def step(k):
                slopes_of(k)
                gather_grads(k, False)

                @pl.when(k > 0)
                def _():
                    hand_on(k)

            loop(first_k, end_k - 1, step)
        slopes_of(end_k - 1)
        if held:
            loop(1, jnp.where(z > 0, end_k - 1, 1), hand_on)
        gather_grads(end_k - 1, True)

        @pl.when(z + end_k <= columns)
        def _():
            hand_on(end_k - 1)

        halve(0, total_turned[:, rows:].astype(low))
        hand_on(0)
        halve(columns, total_turned[:, :rows].astype(low))
        if held:
            loop(1, jnp.where(z > 0, 1, end_k - 1), hand_on)
        swap(columns).wait_recv()
        term_own[...] = term_half[columns, sub] + swap_in[columns].astype(jnp.float32)

    def weight_wait(j):
        push(outgoing.at[j], arrived.at[j], w_send.at[j], w_recv.at[j], across).wait_recv()

    each_other(weight_wait)
    total = terms[me]
    for d in range(1, n):
        total = total + arrived[lax.rem(me + d, n)].astype(jnp.float32)
    grad_weights[0] = total[:, :width]
    grad_weights[1] = total[:, width:]

    targets(1, reach + 1, lambda k: sent(k, toward(k)))
    sent(0, across)
    if n > 1:
        each_other(lambda j: table_copy(j).wait_send())
        loop(0, end_k, lambda k: core(k, mine).wait_send())
        each_other(lambda j: weight_copy(j).wait_send())
        swapped = jnp.where(z + end_k > columns, end_k - 1, end_k)
        loop(0, swapped, lambda k: swap(k).wait_send())
        swap(columns).wait_send()
        loop(0, swapped, lambda k: term_copy(k).wait_send())

        @pl.when(z + end_k > columns)
        def _():
            for s in range(2):
                last_copy(end_k - 1, s).wait_send()

    def take(k):
        push(term_out.at[k], term_in.at[k], d_send.at[k], d_recv.at[k], across).wait_recv()
        term_own[...] += term_in[k].astype(jnp.float32)

    def ends(k):
        return (k > z) & (k == span(lax.rem(z - k + columns, columns)))

    def take_summed(k):
        @pl.when(jnp.logical_not(ends(k)))
        def _():
            take(k)

    def take_last(k):
        @pl.when(ends(k))
        def _():
            for s in range(2):
                push(last_out.at[s], last_in.at[s], l_send.at[s], l_recv.at[s], across).wait_recv()
            grad_feats[0] = (
                term_half[columns, 0] + last_in[0].astype(jnp.float32) + last_in[1].astype(jnp.float32)
            ).astype(grad_feats.dtype)

    take(0)
    targets(1, reach + 1, take_summed)
    turned = term_own[...].T
    grad_feats[0] = turned.astype(grad_feats.dtype)
    term_half[columns, 0] = turned
    targets(1, reach + 1, take_last)


def store(feats_from, weights_from, feats_to, weights_to, sem):
    copies = [
        pltpu.make_async_copy(feats_from, feats_to, sem.at[0]),
        pltpu.make_async_copy(weights_from, weights_to, sem.at[1]),
    ]
    for copy in copies:
        copy.start()
    for copy in copies:
        copy.wait()


def local(feats, grad_msg, w_qk, w_v, pair_slots, counts):
    n = lax.axis_size("img")
    columns = n // 2
    held = columns if columns <= HELD_COLUMNS else 1
    rows, depth = feats.shape[1:]
    width = w_qk.shape[1]
    heads = width // HEAD_DIM
    share = depth // n
    slots = pair_slots.shape[1]
    low, full = jnp.bfloat16, jnp.float32
    vmem = pltpu.VMEM
    dma = pltpu.SemaphoreType.DMA
    results = pl.pallas_call(
        functools.partial(kernel, n),
        out_shape=(
            vmem((1, rows, width), low),
            vmem((2, share, width), full),
        ),
        in_specs=[HBM] * 6,
        out_specs=(VMEM,) * 2,
        scratch_shapes=[
            vmem((rows, depth), low),
            vmem((rows, width), low),
            vmem((columns, rows, depth), low),
            vmem((columns, rows, width), low),
            vmem((2, slots), jnp.int32),
            pltpu.SMEM((1,), jnp.int32),
            vmem((n, 2, LANES), jnp.int32),
            vmem((depth, 2 * width), low),
            vmem((width + depth, depth), low),
            vmem((2 * rows, width), low),
            vmem((2 * rows, width), low),
            vmem((2 * heads * rows, width), low),
            vmem((2 * heads * rows, width), low),
            vmem((width, 2 * rows), low),
            vmem((width, 2 * rows), low),
            vmem((depth, 2 * rows), low),
            vmem((2 * width, 2 * rows), full),
            vmem((depth, 2 * width), full),
            vmem((held, 2 * rows, heads * rows), low),
            vmem((held, 2 * rows, heads * rows), low),
            vmem((held, rows, 2 * heads * rows), low),
            vmem((held, rows, 2 * heads * rows), low),
            vmem((held, width, rows), low),
            vmem((held, width, rows), low),
            vmem((held, depth, rows), low),
            vmem((n, share, 2 * width), full),
            vmem((n, share, 2 * width), low),
            vmem((n, share, 2 * width), low),
            vmem((width, rows), full),
            vmem((2, rows, width), low),
            vmem((2, rows, width), low),
            vmem((columns + 1, 2, width, rows), full),
            vmem((columns, width, rows), low),
            vmem((columns, width, rows), low),
            vmem((columns + 1, width, rows), low),
            vmem((columns + 1, width, rows), low),
            dma((6,)), pltpu.SemaphoreType.REGULAR((n,)),
            dma((columns,)), dma((columns,)), dma((columns,)),
            dma((columns,)), dma((columns,)), dma((columns,)),
            dma((n,)), dma((n,)), dma((n,)), dma((n,)),
            dma((columns,)), dma((columns,)), dma((columns + 1,)), dma((columns + 1,)),
            dma((2,)), dma((2,)),
        ],
        compiler_params=pltpu.CompilerParams(
            collective_id=0, has_side_effects=True, vmem_limit_bytes=60 * 1024 * 1024
        ),
        name="backward",
    )(feats, grad_msg, w_qk, w_v, jnp.transpose(pair_slots, (0, 2, 1)), counts)
    any_space = pl.BlockSpec(memory_space=pltpu.VMEM)
    return pl.pallas_call(
        store,
        out_shape=(
            jax.ShapeDtypeStruct((1, rows, width), low),
            jax.ShapeDtypeStruct((2, share, width), full),
        ),
        in_specs=[any_space] * 2,
        out_specs=(pl.BlockSpec(memory_space=pl.ANY),) * 2,
        scratch_shapes=[dma((2,))],
        name="store",
    )(*(pltpu.with_memory_space_constraint(result, pltpu.VMEM) for result in results))


def solution(mesh):
    in_specs = (
        P(("groups", "img"), None, None),
        P(("groups", "img"), None, "sub"),
        P(None, "sub"),
        P(None, "sub"),
        P(("groups", "img"), None, None),
        P(("groups", "img")),
    )
    out_specs = (P(("groups", "img"), None, "sub"), P("groups", "img", "sub"))
    return jax.shard_map(local, mesh=mesh, in_specs=in_specs, out_specs=out_specs, check_vma=False)
```
